256 devices in a mesh: leaf: 128 (over x, y, z), col: 2 (over core).
Axes of the slice: x: 4, y: 4, z: 8, core: 2. Of those that a mesh axis runs over, the one named last changes fastest.
Arguments:
- coords: float32 [3, 262144], P(None, 'leaf'), may hold values from -6 to 6
- values: float32 [32, 262144], P('col', 'leaf'), may hold values from -6 to 6
- leaf_basis: float32 [1024, 256, 128], P('leaf'), may hold values from -0.375 to 0.375
- leaf_transfer: float32 [1024, 128, 128], P('leaf'), may hold values from -0.1875 to 0.1875
- node_transfer: float32 [128, 128, 128], P('leaf'), may hold values from -0.1875 to 0.1875
- leaf_coupling: float32 [1024, 8, 128, 128], P('leaf', None, 'col'), may hold values from -0.1875 to 0.1875
- node_coupling: float32 [128, 2, 128, 128], P('leaf', None, 'col'), may hold values from -0.375 to 0.375
- top_coupling: float32 [16, 4, 128, 128], P(None, None, 'col'), may hold values from -0.25 to 0.25
- near_list: int32 [1024, 8], P('leaf'), may hold values from -1 to 1023, as said below
- leaf_list: int32 [1024, 8], P('leaf'), may hold values from -1 to 1023, as said below
- node_list: int32 [128, 2], P('leaf'), may hold values from -1 to 127, as said below
- top_list: int32 [16, 4], replicated, may hold values from -1 to 15, as said below
Outputs:
- adjoint_product: float32 [32, 262144], P('col', 'leaf')
The draws below stay inside these ranges and needn't reach their ends.
Inputs may be any that keep to these rules, and one draw needn't show every extreme that they name: `leaf_list`: leaf l names only leaves other than itself on devices l // 8 - 1 to l // 8 + 1 of a Morton order of 8 leaves a device; slot 0 is live, live slots come first, and some leaf fills all 8 slots. `near_list`: leaf l names only leaves (itself allowed) on devices l // 8 - 1 to l // 8 + 1; slot 0 is live, live slots come first, and some leaf fills all 8 slots. `node_list`: node p names only nodes p - 1 and p + 1; slot 0 is live, live slots come first, and some node fills all 2 slots. `top_list`: top node g may name any top node, itself allowed; slot 0 is live, live slots come first, and some top node fills all 4 slots.
All inputs are finite; a program needn't handle non-finite values.
Results may differ from the reference program's by a relative error of at most 0.0003.
Values sent between devices are 32-bit elements; how exact they have to be, the bound alone decides.
A program may use at most 64 MiB of HBM per device.

```python
import jax
import jax.numpy as jnp
from jax import lax

RANK = 128
LEAF_PTS = 256
COLS = 32
LEAF_DEV = 8
SLOTS_NEAR = 8
SLOTS_LEAF = 8
SLOTS_MID = 2
SLOTS_TOP = 4
LEAVES = 1024
POINTS = 262144
NODES1 = 128
NODES2 = 16


def window_list(key, total_rows, slot_count, group_size, with_self):
    indices = jnp.arange(total_rows, dtype=jnp.int32)
    owner_block = indices // group_size
    blocks = total_rows // group_size
    window_start = jnp.maximum(owner_block - 1, 0) * group_size
    window_end = jnp.minimum(owner_block + 2, blocks) * group_size
    window_size = window_end - window_start
    key_live, key_pick, key_full = jax.random.split(key, 3)
    live_count = jax.random.randint(key_live, (total_rows,), 1, slot_count + 1)
    filled = jax.random.randint(key_full, (), 0, total_rows)
    live_count = jnp.where(indices == filled, slot_count, live_count)
    random_pick = jax.random.randint(key_pick, (total_rows, slot_count), 0, 1 << 20)
    if with_self:
        source = window_start[:, None] + random_pick % window_size[:, None]
    else:
        source = window_start[:, None] + random_pick % (window_size[:, None] - 1)
        source = jnp.where(source >= indices[:, None], source + 1, source)
    places = jnp.arange(slot_count, dtype=jnp.int32)[None, :]
    return jnp.where(places < live_count[:, None], source, -1).astype(jnp.int32)


def draw_near_list(key, part):
    return window_list(jax.random.fold_in(key, 11), LEAVES, SLOTS_NEAR, LEAF_DEV, True)


def draw_leaf_list(key, part):
    return window_list(jax.random.fold_in(key, 23), LEAVES, SLOTS_LEAF, LEAF_DEV, False)


def draw_node_list(key, part):
    return window_list(jax.random.fold_in(key, 37), NODES1, SLOTS_MID, 1, False)


def draw_top_list(key, part):
    return window_list(jax.random.fold_in(key, 41), NODES2, SLOTS_TOP, NODES2, True)


def level_of(own_key, shape, pieces, smallest, high):
    def one(dim, shards_of):
        steps = jax.random.uniform(jax.random.fold_in(jax.random.fold_in(own_key, 6), dim), (shards_of,), jnp.float32, smallest / len(pieces), high / len(pieces))
        return jnp.repeat(jnp.exp(steps), shape[dim] // shards_of).reshape((-1,) + (1,) * (len(shape) - dim - 1))

    level = one(*pieces[0])
    for cut in pieces[1:]:
        level = level * one(*cut)
    return level


def gaussian(stream_key, extent, spread, limit, cuts=(), kind=jnp.bfloat16):
    values = spread * jax.random.normal(stream_key, extent, jnp.float32)
    if cuts:
        values = values * level_of(stream_key, extent, cuts, -0.22, 0.18)
    return jnp.clip(values, -limit, limit).astype(kind)


def setup_inputs(seed: int = 0) -> dict:
    streams_of = jax.random.split(jax.random.key(seed), 13)
    coords = gaussian(streams_of[0], (3, POINTS), 1.0, 6.0, ((1, 128),), jnp.float32)
    values = gaussian(streams_of[1], (COLS, POINTS), 1.0, 6.0, ((0, 2), (1, 128)), jnp.float32)
    leaf_basis = gaussian(streams_of[2], (LEAVES, LEAF_PTS, RANK), LEAF_PTS ** -0.5, 0.375, ((0, 128),), jnp.float32)
    leaf_transfer = gaussian(streams_of[3], (LEAVES, RANK, RANK), (8 * RANK) ** -0.5, 0.1875, ((0, 128),), jnp.float32)
    node_transfer = gaussian(streams_of[4], (NODES1, RANK, RANK), (8 * RANK) ** -0.5, 0.1875, ((0, 128),), jnp.float32)
    leaf_coupling = gaussian(streams_of[5], (LEAVES, SLOTS_LEAF, RANK, RANK), (SLOTS_LEAF * RANK) ** -0.5, 0.1875, ((0, 128), (2, 2)), jnp.float32)
    node_coupling = gaussian(streams_of[6], (NODES1, SLOTS_MID, RANK, RANK), (SLOTS_MID * RANK) ** -0.5, 0.375, ((0, 128), (2, 2)), jnp.float32)
    top_coupling = gaussian(streams_of[7], (NODES2, SLOTS_TOP, RANK, RANK), (SLOTS_TOP * RANK) ** -0.5, 0.25, ((2, 2),), jnp.float32)
    near_list = draw_near_list(jax.random.fold_in(streams_of[12], 71), 0)
    leaf_list = draw_leaf_list(jax.random.fold_in(streams_of[12], 71), 0)
    node_list = draw_node_list(jax.random.fold_in(streams_of[12], 71), 0)
    top_list = draw_top_list(jax.random.fold_in(streams_of[12], 71), 0)
    return {"coords": coords, "values": values, "leaf_basis": leaf_basis, "leaf_transfer": leaf_transfer, "node_transfer": node_transfer, "leaf_coupling": leaf_coupling, "node_coupling": node_coupling, "top_coupling": top_coupling, "near_list": near_list, "leaf_list": leaf_list, "node_list": node_list, "top_list": top_list}


SOFTENING = 0.01

def kernel_tile(target, source):
    offset_sq = lax.optimization_barrier(jnp.sum((target[:, :, None] - source[:, None, :]) ** 2, axis=0))
    return 1.0 / (jnp.sqrt(jnp.float32(LEAF_PTS)) * jnp.sqrt(offset_sq + SOFTENING))

def couple(blocks, lists, moments):
    live_mask = (lists >= 0).astype(jnp.float32)
    picked = moments[jnp.maximum(lists, 0)] * live_mask[:, :, None, None]
    return jnp.einsum('nsca,nsab->ncb', picked, blocks, precision=lax.Precision.HIGHEST)

def reference(coords, values, leaf_basis, leaf_transfer, node_transfer, leaf_coupling, node_coupling, top_coupling, near_list, leaf_list, node_list, top_list):
    leaf_values = values.reshape(COLS, LEAVES, LEAF_PTS)
    high = lax.Precision.HIGHEST
    leaf_moments = jnp.einsum('lpr,clp->lcr', leaf_basis, leaf_values, precision=high)
    node_moments = jnp.einsum('lab,lca->lcb', leaf_transfer, leaf_moments, precision=high)
    node_moments = node_moments.reshape(NODES1, LEAF_DEV, COLS, RANK).sum(axis=1)
    top_moments = jnp.einsum('nab,nca->ncb', node_transfer, node_moments, precision=high)
    top_moments = top_moments.reshape(NODES2, 8, COLS, RANK).sum(axis=1)
    top_local = couple(top_coupling, top_list, top_moments)
    node_local = couple(node_coupling, node_list, node_moments) + jnp.einsum('nab,ncb->nca', node_transfer, jnp.repeat(top_local, 8, axis=0), precision=high)
    leaf_local = couple(leaf_coupling, leaf_list, leaf_moments) + jnp.einsum('lab,lcb->lca', leaf_transfer, jnp.repeat(node_local, LEAF_DEV, axis=0), precision=high)
    far_field = jnp.einsum('lpr,lcr->clp', leaf_basis, leaf_local, precision=high)
    leaf_points = coords.reshape(3, LEAVES, LEAF_PTS)

    def one_leaf(leaf_index):
        target = leaf_points[:, leaf_index]
        listed = near_list[leaf_index]
        near_sum = jnp.zeros((COLS, LEAF_PTS), jnp.float32)
        for slot_index in range(SLOTS_NEAR):
            source_leaf = jnp.maximum(listed[slot_index], 0)
            live_mask = (listed[slot_index] >= 0).astype(jnp.float32)
            kernel = kernel_tile(target, leaf_points[:, source_leaf])
            near_sum = near_sum + live_mask * jnp.dot(leaf_values[:, source_leaf], kernel.T, precision=high)
        return near_sum
    near_field = lax.map(one_leaf, jnp.arange(LEAVES, dtype=jnp.int32))
    near_field = jnp.transpose(near_field, (1, 0, 2))
    return (near_field + far_field).reshape(COLS, POINTS)
```

```python
import functools

import jax
import jax.numpy as jnp
from jax import lax
from jax.experimental import pallas as pl
from jax.experimental.pallas import tpu as pltpu
from jax.sharding import PartitionSpec as P

SOFTENING = 0.01
F32, BF16 = jnp.float32, jnp.bfloat16
MESH = pl.DeviceIdType.MESH
NN = (((1,), (0,)), ((), ()))
NT = (((1,), (1,)), ((), ()))


def mm(a, b, dims):
    return lax.dot_general(a, b, dims, preferred_element_type=F32)


def split(x):
    hi = x.astype(BF16)
    return hi, (x - hi.astype(F32)).astype(BF16)


def stacked(x):
    return jnp.concatenate(split(x), axis=0)


def dot3(x2, yh, yl, dims):
    m = x2.shape[0] // 2
    both = mm(x2, yh, dims)
    return both[:m] + both[m:] + mm(x2[:m], yl, dims)


def kernel(
    near_ref, leaf_ref, node_ref, top_ref, coords,
    values_hbm, basis_hbm, ltr_hbm, ntr_hbm, lcp_hbm, ncp_hbm, tcp_hbm,
    out,
    vals, ev, cs, vs, bx, em, en, zb, tb, sm, sn, sc, st,
    basis, ltr, ntr, lcp, ncp, tcp, bh, bl, lth, ltl, nth, ntl,
    ox, sx, rx, sp, rp,
    local_sem, v_send, v_recv, c_send, c_recv, m_send, m_recv, n_send, n_recv,
    z_send, z_recv, t_send, t_recv, x_send, x_recv,
):
    leaves, chips = 8, 128
    cols = vals.shape[0]
    d, c = lax.axis_index("leaf"), lax.axis_index("col")
    o = 1 - c
    z, g = lax.rem(d, 8), lax.div(d, 8)
    after, before = lax.rem(d + 1, chips), lax.rem(d + chips - 1, chips)

    def fetch(i, src, dst):
        copy = pltpu.make_async_copy(src, dst, local_sem.at[i])
        copy.start()
        return copy

    get_values = fetch(0, values_hbm, vals)
    get_basis = fetch(1, basis_hbm, basis)
    get_ltr = fetch(2, ltr_hbm, ltr)
    get_ntr = fetch(3, ntr_hbm, ntr)
    get_lcp = fetch(4, lcp_hbm, lcp)
    get_ncp = fetch(5, ncp_hbm, ncp)
    get_tcp = fetch(6, tcp_hbm.at[g], tcp)

    barrier = pltpu.get_barrier_semaphore()

    def greet(leaf, col):
        pl.semaphore_signal(barrier, inc=1, device_id=(leaf, col), device_id_type=MESH)

    greet(d, o)
    for h in range(2):
        greet(after, h)
        greet(before, h)
        for k in range(1, 8):
            greet(g * 8 + lax.rem(z + k, 8), h)
    for k in range(1, 16):
        greet(lax.rem(g + k, 16) * 8 + z, c)

    def remote(src, dst, ssem, rsem, leaf, col):
        return pltpu.make_async_remote_copy(
            src_ref=src, dst_ref=dst, send_sem=ssem, recv_sem=rsem,
            device_id=(leaf, col), device_id_type=MESH,
        )

    zero8 = jnp.zeros((8, 128), F32)
    for l in range(leaves):
        for h in range(2):
            start = l * 256 + h * 128
            cs[leaves + l, 3 * h : 3 * h + 3, :] = coords[:, start : start + 128]
        cs[leaves + l, 6:8, :] = zero8[:2]
    cs[24] = zero8
    vs[24] = jnp.zeros((2 * cols, 256), BF16)
    for s in range(2):
        em[s, 24] = zero8
        en[s, 3] = zero8
        tb[16, s] = zero8
    get_values.wait()
    for l in range(leaves):
        vs[leaves + l] = stacked(vals[:, l * 256 : (l + 1) * 256])

    pl.semaphore_wait(barrier, 34)
    sends = []

    def send(*args):
        copy = remote(*args)
        copy.start()
        sends.append(copy)

    for q, leaf in ((0, after), (1, before)):
        send(vals, ev.at[q], v_send.at[q], v_recv.at[q], leaf, c)
        send(cs.at[pl.ds(leaves, leaves)], cs.at[pl.ds(16 * q, leaves)], c_send.at[q], c_recv.at[q], leaf, c)

    low = lax.broadcasted_iota(jnp.int32, (8, 128), 1) < 64

    def half(x, h):
        a, b = x[:8], x[8:]
        return jnp.where(low, a, pltpu.roll(b, 64, 1)) if h == 0 else jnp.where(low, pltpu.roll(a, 64, 1), b)

    get_basis.wait()
    get_ltr.wait()
    get_ntr.wait()
    nth[...], ntl[...] = split(ntr[0])
    node = None
    for l in range(leaves):
        hi, lo = split(basis[l])
        bh[l], bl[l] = hi, lo
        moments = dot3(vs[leaves + l], hi, lo, NN)
        for h in range(2):
            sm[h, l] = half(moments, h)
        thi, tlo = split(ltr[l])
        lth[l], ltl[l] = thi, tlo
        term = dot3(stacked(moments), thi, tlo, NN)
        node = term if node is None else node + term
    contrib = dot3(stacked(node), nth[...], ntl[...], NN)
    for h in range(2):
        sn[h] = half(node, h)
        sc[h] = half(contrib, h)

    send(sc.at[o], zb.at[0, c], z_send.at[0, o], z_recv.at[0, c], d, o)
    for k in range(1, 8):
        for h in range(2):
            send(sc.at[h], zb.at[k, c], z_send.at[k, h], z_recv.at[k, c], g * 8 + lax.rem(z + k, 8), h)
    zb[0, c] = sc[c]
    send(sm.at[o], em.at[c, pl.ds(leaves, leaves)], m_send.at[2, o], m_recv.at[1, c], d, o)
    send(sn.at[o], en.at[c, 1], n_send.at[2, o], n_recv.at[1, c], d, o)
    for q, leaf in ((0, after), (1, before)):
        for h in range(2):
            send(sn.at[h], en.at[c, 2 * q], n_send.at[q, h], n_recv.at[2 * q, c], leaf, h)
            send(sm.at[h], em.at[c, pl.ds(16 * q, leaves)], m_send.at[q, h], m_recv.at[2 * q, c], leaf, h)
    em[c, pl.ds(leaves, leaves)] = sm[c]
    en[c, 1] = sn[c]

    for q in range(2):
        remote(vals, ev.at[q], v_send.at[q], v_recv.at[q], after, c).wait_recv()
        mine = cs.at[pl.ds(16 * q, leaves)]
        remote(mine, mine, c_send.at[q], c_recv.at[q], after, c).wait_recv()
        for l in range(leaves):
            vs[16 * q + l] = stacked(ev[q, :, l * 256 : (l + 1) * 256])

    def source(v, per, none):
        return jnp.where(v >= 0, jnp.clip(v - (d - 1) * per, 0, none - 1), none)

    def near(l, carry):
        points = cs[leaves + l].T
        for k in range(3):
            bx[k, 0:128, :] = jnp.broadcast_to(points[:, k : k + 1], (128, 128))
            bx[k, 128:256, :] = jnp.broadcast_to(points[:, 3 + k : 4 + k], (128, 128))
        total = None
        for j in range(8):
            i = source(near_ref[l, j], leaves, 24)
            rows = cs[i]
            his, los = [], []
            for h in range(2):
                r2 = None
                for k in range(3):
                    e = bx[k] - rows[3 * h + k : 3 * h + k + 1, :]
                    r2 = e * e if r2 is None else r2 + e * e
                hi, lo = split(lax.rsqrt(r2 + SOFTENING))
                his.append(hi)
                los.append(lo)
            term = dot3(vs[i], jnp.concatenate(his, 1), jnp.concatenate(los, 1), NT)
            total = term if total is None else total + term
        out[:, pl.ds(pl.multiple_of(l * 256, 256), 256)] = total * (1.0 / 16.0)
        return carry

    lax.fori_loop(0, 3, near, 0)

    for k in range(8):
        for s in range(2):
            if k == 0:
                continue
            remote(sc.at[0], zb.at[k, s], z_send.at[k, s], z_recv.at[k, s], d, o).wait_recv()
    remote(sc.at[0], zb.at[0, o], z_send.at[0, o], z_recv.at[0, o], d, o).wait_recv()
    total = zb[0]
    for k in range(1, 8):
        total = total + zb[k]
    st[...] = total
    for k in range(1, 16):
        send(st, tb.at[g], t_send.at[k], t_recv.at[k], lax.rem(g + k, 16) * 8 + z, c)
    tb[g] = total

    def paired(load, i, j):
        rows = []
        for s in range(2):
            a, b = load(s, i), load(s, j)
            rows += [jnp.where(low, a, pltpu.roll(b, 64, 1)), jnp.where(low, pltpu.roll(a, 64, 1), b)]
        return jnp.concatenate(rows, 0)

    def coupled(load, index, blocks):
        slots = blocks.shape[0]
        picked = jnp.concatenate([paired(load, index(j), index(j + 1)) for j in range(0, slots, 2)], 1)
        return dot3(stacked(picked), *split(blocks.reshape(slots * 64, 128)), NN)

    for h in range(2):
        for q in (0, 2):
            remote(sm.at[h], em.at[h, pl.ds(8 * q, leaves)], m_send.at[0, h], m_recv.at[q, h], d, o).wait_recv()
            remote(sn.at[h], en.at[h, q], n_send.at[0, h], n_recv.at[q, h], d, o).wait_recv()
    remote(sm.at[o], em.at[o, pl.ds(leaves, leaves)], m_send.at[2, o], m_recv.at[1, o], d, o).wait_recv()
    remote(sn.at[o], en.at[o, 1], n_send.at[2, o], n_recv.at[1, o], d, o).wait_recv()
    get_lcp.wait()
    get_ncp.wait()
    get_tcp.wait()
    first = jnp.full((cols, 128), c, jnp.int32) == 0

    def keep(i, both):
        a, b = both[:cols], both[cols:]
        ox[i] = jnp.where(first, a, b)
        sx[i] = jnp.where(first, b, a)

    for l in range(leaves):
        keep(l, coupled(lambda s, i: em[s, i], lambda j: source(leaf_ref[l, j], leaves, 24), lcp[l]))
    keep(leaves, coupled(lambda s, i: en[s, i], lambda j: source(node_ref[0, j], 1, 3), ncp[0]))
    send(sx, rx, x_send.at[0], x_recv.at[0], d, o)

    lax.fori_loop(3, 8, near, 0)

    for k in range(1, 16):
        remote(st, tb.at[g], t_send.at[k], t_recv.at[k], d, o).wait_recv()

    def top_index(j):
        v = top_ref[g, j]
        return jnp.where(v >= 0, v, 16)

    both = coupled(lambda s, i: tb[i, s], top_index, tcp[...])
    a, b = both[:cols], both[cols:]
    sp[...] = jnp.where(first, b, a)
    send(sp, rp, x_send.at[1], x_recv.at[1], d, o)
    remote(sx, rx, x_send.at[0], x_recv.at[0], d, o).wait_recv()
    remote(sp, rp, x_send.at[1], x_recv.at[1], d, o).wait_recv()
    top_local = jnp.where(first, a, b) + rp[...]
    node_local = ox[leaves] + rx[leaves] + dot3(stacked(top_local), nth[...], ntl[...], NT)
    node2 = stacked(node_local)
    for l in range(leaves):
        leaf_local = ox[l] + rx[l] + dot3(node2, lth[l], ltl[l], NT)
        far = dot3(stacked(leaf_local), bh[l], bl[l], NT)
        out[:, l * 256 : (l + 1) * 256] = out[:, l * 256 : (l + 1) * 256] + far
    for copy in sends:
        copy.wait_send()


def body(
    coords, values, leaf_basis, leaf_transfer, node_transfer, leaf_coupling, node_coupling, top_coupling,
    near_list, leaf_list, node_list, top_list,
):
    cols = values.shape[0]
    any_ref = pl.BlockSpec(memory_space=pl.ANY)
    smem = pl.BlockSpec(memory_space=pltpu.SMEM)
    vmem = pl.BlockSpec(memory_space=pltpu.VMEM)
    dma = pltpu.SemaphoreType.DMA
    return pl.pallas_call(
        kernel,
        out_shape=jax.ShapeDtypeStruct(values.shape, F32),
        in_specs=[smem] * 4 + [vmem] + [any_ref] * 7,
        out_specs=vmem,
        scratch_shapes=[
            pltpu.VMEM((cols, 2048), F32),
            pltpu.VMEM((2, cols, 2048), F32),
            pltpu.VMEM((25, 8, 128), F32),
            pltpu.VMEM((25, 2 * cols, 256), BF16),
            pltpu.VMEM((3, 256, 128), F32),
            pltpu.VMEM((2, 25, 8, 128), F32),
            pltpu.VMEM((2, 4, 8, 128), F32),
            pltpu.VMEM((8, 2, 8, 128), F32),
            pltpu.VMEM((17, 2, 8, 128), F32),
            pltpu.VMEM((2, 8, 8, 128), F32),
            pltpu.VMEM((2, 8, 128), F32),
            pltpu.VMEM((2, 8, 128), F32),
            pltpu.VMEM((2, 8, 128), F32),
            pltpu.VMEM((8, 256, 128), F32),
            pltpu.VMEM((8, 128, 128), F32),
            pltpu.VMEM((1, 128, 128), F32),
            pltpu.VMEM((8, 8, 64, 128), F32),
            pltpu.VMEM((1, 2, 64, 128), F32),
            pltpu.VMEM((4, 64, 128), F32),
            pltpu.VMEM((8, 256, 128), BF16),
            pltpu.VMEM((8, 256, 128), BF16),
            pltpu.VMEM((8, 128, 128), BF16),
            pltpu.VMEM((8, 128, 128), BF16),
            pltpu.VMEM((128, 128), BF16),
            pltpu.VMEM((128, 128), BF16),
            pltpu.VMEM((9, cols, 128), F32),
            pltpu.VMEM((9, cols, 128), F32),
            pltpu.VMEM((9, cols, 128), F32),
            pltpu.VMEM((cols, 128), F32),
            pltpu.VMEM((cols, 128), F32),
            dma((7,)),
            dma((2,)), dma((2,)), dma((2,)), dma((2,)),
            dma((3, 2)), dma((3, 2)), dma((3, 2)), dma((3, 2)),
            dma((8, 2)), dma((8, 2)), dma((16,)), dma((16,)),
            dma((2,)), dma((2,)),
        ],
        compiler_params=pltpu.CompilerParams(collective_id=0, has_side_effects=True),
    )(
        near_list, leaf_list, node_list, top_list, coords, values,
        leaf_basis, leaf_transfer, node_transfer, leaf_coupling, node_coupling, top_coupling,
    )


def solution(mesh):
    in_specs = (
        P(None, "leaf"),
        P("col", "leaf"),
        P("leaf", None, None),
        P("leaf", None, None),
        P("leaf", None, None),
        P("leaf", None, "col", None),
        P("leaf", None, "col", None),
        P(None, None, "col", None),
        P("leaf", None),
        P("leaf", None),
        P("leaf", None),
        P(),
    )
    return jax.shard_map(body, mesh=mesh, in_specs=in_specs, out_specs=P("col", "leaf"), check_vma=False)
```

```python
import functools

import jax
import jax.numpy as jnp
from jax import lax
from jax.experimental import pallas as pl
from jax.experimental.pallas import tpu as pltpu
from jax.sharding import PartitionSpec as P

SOFTENING = 0.01
F32, BF16 = jnp.float32, jnp.bfloat16
MESH = pl.DeviceIdType.MESH
NN = (((1,), (0,)), ((), ()))
NT = (((1,), (1,)), ((), ()))


def mm(a, b, dims):
    return lax.dot_general(a, b, dims, preferred_element_type=F32)


def split(x):
    hi = x.astype(BF16)
    return hi, (x - hi.astype(F32)).astype(BF16)


def stacked(x):
    return jnp.concatenate(split(x), axis=0)


def dot3(x2, yh, yl, dims):
    m = x2.shape[0] // 2
    both = mm(x2, yh, dims)
    return both[:m] + both[m:] + mm(x2[:m], yl, dims)


def kernel(
    near_hbm, leaf_hbm, node_hbm, top_hbm, coords_hbm,
    values_hbm, basis_hbm, ltr_hbm, ntr_hbm, lcp_hbm, ncp_hbm, tcp_hbm,
    out,
    near_ref, leaf_ref, node_ref, top_ref, coords,
    vals, ev, cs, vs, bx, em, en, zb, tb, sm, sn, sc, st,
    basis, ltr, ntr, lcp, ncp, tcp, bh, bl, lth, ltl, nth, ntl, tth, ttl,
    ox, sx, rx,
    local_sem, v_send, v_recv, c_send, c_recv, m_send, m_recv, n_send, n_recv,
    z_send, z_recv, t_send, t_recv, x_send, x_recv,
):
    leaves, chips = 8, 128
    cols = vals.shape[0]
    d, c = lax.axis_index("leaf"), lax.axis_index("col")
    o = 1 - c
    z, g = lax.rem(d, 8), lax.div(d, 8)
    after, before = lax.rem(d + 1, chips), lax.rem(d + chips - 1, chips)

    def fetch(i, src, dst):
        copy = pltpu.make_async_copy(src, dst, local_sem.at[i])
        copy.start()
        return copy

    get_values = fetch(0, values_hbm, vals)
    quarters = [pl.ds(4 * i, 4) for i in range(2)]
    get_basis = [fetch(1 + i, basis_hbm.at[q], basis.at[q]) for i, q in enumerate(quarters)]
    get_ltr = fetch(3, ltr_hbm, ltr)
    get_ntr = fetch(4, ntr_hbm, ntr)
    get_coords = fetch(5, coords_hbm, coords)
    get_tcp = fetch(6, tcp_hbm.at[g], tcp.at[c])
    get_lists = [
        fetch(7 + i, src, dst)
        for i, (src, dst) in enumerate(
            ((near_hbm, near_ref), (leaf_hbm, leaf_ref), (node_hbm, node_ref), (top_hbm, top_ref))
        )
    ]
    get_lcp = fetch(11, lcp_hbm, lcp)
    get_ncp = fetch(12, ncp_hbm, ncp)

    barrier = pltpu.get_barrier_semaphore()

    def greet(leaf, col):
        pl.semaphore_signal(barrier, inc=1, device_id=(leaf, col), device_id_type=MESH)

    for k in range(1, 8):
        greet(g * 8 + lax.rem(z + k, 8), c)
    for h in range(2):
        greet(after, h)
        greet(before, h)
    greet(d, o)
    for k in range(1, 16):
        greet(lax.rem(g + k, 16) * 8 + z, c)

    def remote(src, dst, ssem, rsem, leaf, col):
        return pltpu.make_async_remote_copy(
            src_ref=src, dst_ref=dst, send_sem=ssem, recv_sem=rsem,
            device_id=(leaf, col), device_id_type=MESH,
        )

    sends = []

    def send(*args):
        copy = remote(*args)
        copy.start()
        sends.append(copy)

    get_values.wait()
    for l in range(leaves):
        vs[leaves + l] = stacked(vals[:, l * 256 : (l + 1) * 256])
    moments = []
    for l in range(leaves):
        if l % 4 == 0:
            get_basis[l // 4].wait()
        hi, lo = split(basis[l])
        bh[l], bl[l] = hi, lo
        moments.append(dot3(vs[leaves + l], hi, lo, NN))
    get_ltr.wait()
    lth[...], ltl[...] = split(ltr[...])
    down = (leaves * 128, 128)
    node = dot3(stacked(jnp.concatenate(moments, 1)), lth[...].reshape(down), ltl[...].reshape(down), NN)
    get_ntr.wait()
    nth[...], ntl[...] = split(ntr[0])
    contrib = dot3(stacked(node), nth[...], ntl[...], NN)
    sc[...] = contrib
    pl.semaphore_wait(barrier, 27)
    for k in range(1, 8):
        send(sc, zb.at[k], z_send.at[k], z_recv.at[k], g * 8 + lax.rem(z + k, 8), c)

    low = lax.broadcasted_iota(jnp.int32, (8, 128), 1) < 64

    def half(x, h):
        a, b = x[:8], x[8:]
        return jnp.where(low, a, pltpu.roll(b, 64, 1)) if h == 0 else jnp.where(low, pltpu.roll(a, 64, 1), b)

    for h in range(2):
        sn[h] = half(node, h)
        for l in range(leaves):
            sm[h, l] = half(moments[l], h)
    own = pl.ds(leaves, leaves)
    get_tcp.wait()
    send(tcp.at[c], tcp.at[c], x_send.at[1], x_recv.at[1], d, o)
    send(sm.at[o], em.at[c, own], m_send.at[2, o], m_recv.at[1, c], d, o)
    send(sn.at[o], en.at[c, 1], n_send.at[2, o], n_recv.at[1, c], d, o)
    for q, leaf in ((0, after), (1, before)):
        for h in range(2):
            send(sn.at[h], en.at[c, 2 * q], n_send.at[q, h], n_recv.at[2 * q, c], leaf, h)
            send(sm.at[h], em.at[c, pl.ds(16 * q, leaves)], m_send.at[q, h], m_recv.at[2 * q, c], leaf, h)
    em[c, own] = sm[c]
    en[c, 1] = sn[c]

    zero8 = jnp.zeros((8, 128), F32)
    get_coords.wait()
    for l in range(leaves):
        for h in range(2):
            start = l * 256 + h * 128
            cs[leaves + l, 3 * h : 3 * h + 3, :] = coords[:, start : start + 128]
        cs[leaves + l, 6:8, :] = zero8[:2]
    for q, leaf in ((0, after), (1, before)):
        send(vals, ev.at[q], v_send.at[q], v_recv.at[q], leaf, c)
        send(cs.at[own], cs.at[pl.ds(16 * q, leaves)], c_send.at[q], c_recv.at[q], leaf, c)
    cs[24] = zero8
    vs[24] = jnp.zeros((2 * cols, 256), BF16)
    tb[16] = jnp.zeros((cols, 128), F32)
    for s in range(2):
        em[s, 24] = zero8
        en[s, 3] = zero8

    total = contrib
    for k in range(1, 8):
        remote(sc, zb.at[k], z_send.at[k], z_recv.at[k], d, o).wait_recv()
    for k in range(1, 8):
        total = total + zb[k]
    st[...] = total
    for k in range(1, 16):
        send(st, tb.at[g], t_send.at[k], t_recv.at[k], lax.rem(g + k, 16) * 8 + z, c)
    tb[g] = total

    def source(v, first, none):
        return jnp.where(v >= 0, jnp.clip(v - first, 0, none - 1), none)

    def paired(load, i, j):
        rows = []
        for s in range(2):
            a, b = load(s, i), load(s, j)
            rows += [jnp.where(low, a, pltpu.roll(b, 64, 1)), jnp.where(low, pltpu.roll(a, 64, 1), b)]
        return jnp.concatenate(rows, 0)

    def coupled(load, index, blocks):
        slots = blocks.shape[0]
        picked = jnp.concatenate([paired(load, index(j), index(j + 1)) for j in range(0, slots, 2)], 1)
        return dot3(stacked(picked), *split(blocks.reshape(slots * 64, 128)), NN)

    for h in range(2):
        for q in (0, 2):
            remote(sm.at[h], em.at[h, pl.ds(8 * q, leaves)], m_send.at[0, h], m_recv.at[q, h], d, o).wait_recv()
            remote(sn.at[h], en.at[h, q], n_send.at[0, h], n_recv.at[q, h], d, o).wait_recv()
    remote(sm.at[o], em.at[o, own], m_send.at[2, o], m_recv.at[1, o], d, o).wait_recv()
    remote(sn.at[o], en.at[o, 1], n_send.at[2, o], n_recv.at[1, o], d, o).wait_recv()
    for copy in (*get_lists, get_lcp, get_ncp):
        copy.wait()
    first = jnp.full((cols, 128), c, jnp.int32) == 0

    def keep(i, both):
        a, b = both[:cols], both[cols:]
        ox[i] = jnp.where(first, a, b)
        sx[i] = jnp.where(first, b, a)

    for l in range(leaves):
        keep(l, coupled(lambda s, i: em[s, i], lambda j: source(leaf_ref[l, j], (d - 1) * leaves, 24), lcp[l]))
    keep(leaves, coupled(lambda s, i: en[s, i], lambda j: source(node_ref[0, j], d - 1, 3), ncp[0]))
    send(sx, rx, x_send.at[0], x_recv.at[0], d, o)
    remote(tcp.at[o], tcp.at[o], x_send.at[1], x_recv.at[1], d, o).wait_recv()
    for j in range(4):
        for h in range(2):
            rows = pl.ds(j * 128 + h * 64, 64)
            tth[rows], ttl[rows] = split(tcp[h, j])

    for q in range(2):
        remote(vals, ev.at[q], v_send.at[q], v_recv.at[q], after, c).wait_recv()
        mine = cs.at[pl.ds(16 * q, leaves)]
        remote(mine, mine, c_send.at[q], c_recv.at[q], after, c).wait_recv()
        for l in range(leaves):
            vs[16 * q + l] = stacked(ev[q, :, l * 256 : (l + 1) * 256])

    def near(l, carry):
        points = cs[leaves + l].T
        for k in range(3):
            bx[k, 0:128, :] = jnp.broadcast_to(points[:, k : k + 1], (128, 128))
            bx[k, 128:256, :] = jnp.broadcast_to(points[:, 3 + k : 4 + k], (128, 128))
        total = None
        for j in range(8):
            i = source(near_ref[l, j], (d - 1) * leaves, 24)
            rows = cs[i]
            his, los = [], []
            for h in range(2):
                r2 = None
                for k in range(3):
                    e = bx[k] - rows[3 * h + k : 3 * h + k + 1, :]
                    r2 = e * e if r2 is None else r2 + e * e
                hi, lo = split(lax.rsqrt(r2 + SOFTENING))
                his.append(hi)
                los.append(lo)
            term = dot3(vs[i], jnp.concatenate(his, 1), jnp.concatenate(los, 1), NT)
            total = term if total is None else total + term
        out[:, pl.ds(pl.multiple_of(l * 256, 256), 256)] = total * (1.0 / 16.0)
        return carry

    lax.fori_loop(0, 8, near, 0)

    remote(sx, rx, x_send.at[0], x_recv.at[0], d, o).wait_recv()
    for k in range(1, 16):
        remote(st, tb.at[g], t_send.at[k], t_recv.at[k], d, o).wait_recv()
    picked = jnp.concatenate([tb[source(top_ref[j, g], 0, 16)] for j in range(4)], 1)
    top_local = dot3(stacked(picked), tth[...], ttl[...], NN)
    node_local = ox[leaves] + rx[leaves] + dot3(stacked(top_local), nth[...], ntl[...], NT)
    node2 = stacked(node_local)
    for l in range(leaves):
        leaf_local = ox[l] + rx[l] + dot3(node2, lth[l], ltl[l], NT)
        far = dot3(stacked(leaf_local), bh[l], bl[l], NT)
        out[:, l * 256 : (l + 1) * 256] = out[:, l * 256 : (l + 1) * 256] + far
    for copy in sends:
        copy.wait_send()


def body(
    coords, values, leaf_basis, leaf_transfer, node_transfer, leaf_coupling, node_coupling, top_coupling,
    near_list, leaf_list, node_list, top_list,
):
    cols = values.shape[0]
    any_ref = pl.BlockSpec(memory_space=pl.ANY)
    vmem = pl.BlockSpec(memory_space=pltpu.VMEM)
    dma = pltpu.SemaphoreType.DMA
    return pl.pallas_call(
        kernel,
        out_shape=jax.ShapeDtypeStruct(values.shape, F32),
        in_specs=[any_ref] * 12,
        out_specs=vmem,
        scratch_shapes=[
            pltpu.SMEM((8, 8), jnp.int32),
            pltpu.SMEM((8, 8), jnp.int32),
            pltpu.SMEM((1, 2), jnp.int32),
            pltpu.SMEM((4, 16), jnp.int32),
            pltpu.VMEM((3, 2048), F32),
            pltpu.VMEM((cols, 2048), F32),
            pltpu.VMEM((2, cols, 2048), F32),
            pltpu.VMEM((25, 8, 128), F32),
            pltpu.VMEM((25, 2 * cols, 256), BF16),
            pltpu.VMEM((3, 256, 128), F32),
            pltpu.VMEM((2, 25, 8, 128), F32),
            pltpu.VMEM((2, 4, 8, 128), F32),
            pltpu.VMEM((8, cols, 128), F32),
            pltpu.VMEM((17, cols, 128), F32),
            pltpu.VMEM((2, 8, 8, 128), F32),
            pltpu.VMEM((2, 8, 128), F32),
            pltpu.VMEM((cols, 128), F32),
            pltpu.VMEM((cols, 128), F32),
            pltpu.VMEM((8, 256, 128), F32),
            pltpu.VMEM((8, 128, 128), F32),
            pltpu.VMEM((1, 128, 128), F32),
            pltpu.VMEM((8, 8, 64, 128), F32),
            pltpu.VMEM((1, 2, 64, 128), F32),
            pltpu.VMEM((2, 4, 64, 128), F32),
            pltpu.VMEM((8, 256, 128), BF16),
            pltpu.VMEM((8, 256, 128), BF16),
            pltpu.VMEM((8, 128, 128), BF16),
            pltpu.VMEM((8, 128, 128), BF16),
            pltpu.VMEM((128, 128), BF16),
            pltpu.VMEM((128, 128), BF16),
            pltpu.VMEM((512, 128), BF16),
            pltpu.VMEM((512, 128), BF16),
            pltpu.VMEM((9, cols, 128), F32),
            pltpu.VMEM((9, cols, 128), F32),
            pltpu.VMEM((9, cols, 128), F32),
            dma((13,)),
            dma((2,)), dma((2,)), dma((2,)), dma((2,)),
            dma((3, 2)), dma((3, 2)), dma((3, 2)), dma((3, 2)),
            dma((8,)), dma((8,)), dma((16,)), dma((16,)),
            dma((2,)), dma((2,)),
        ],
        compiler_params=pltpu.CompilerParams(collective_id=0, has_side_effects=True),
    )(
        near_list, leaf_list, node_list, top_list.T, coords, values,
        leaf_basis, leaf_transfer, node_transfer, leaf_coupling, node_coupling, top_coupling,
    )


def solution(mesh):
    in_specs = (
        P(None, "leaf"),
        P("col", "leaf"),
        P("leaf", None, None),
        P("leaf", None, None),
        P("leaf", None, None),
        P("leaf", None, "col", None),
        P("leaf", None, "col", None),
        P(None, None, "col", None),
        P("leaf", None),
        P("leaf", None),
        P("leaf", None),
        P(),
    )
    return jax.shard_map(body, mesh=mesh, in_specs=in_specs, out_specs=P("col", "leaf"), check_vma=False)
```

```python
import functools

import jax
import jax.numpy as jnp
from jax import lax
from jax.experimental import pallas as pl
from jax.experimental.pallas import tpu as pltpu
from jax.sharding import PartitionSpec as P

SOFTENING = 0.01
AHEAD = 3
F32, BF16 = jnp.float32, jnp.bfloat16
MESH = pl.DeviceIdType.MESH
NN = (((1,), (0,)), ((), ()))
NT = (((1,), (1,)), ((), ()))


def mm(a, b, dims):
    return lax.dot_general(a, b, dims, preferred_element_type=F32)


def split(x):
    hi = x.astype(BF16)
    return hi, (x - hi.astype(F32)).astype(BF16)


def stacked(x):
    return jnp.concatenate(split(x), axis=0)


def dot3(x2, yh, yl, dims):
    m = x2.shape[0] // 2
    both = mm(x2, yh, dims)
    return both[:m] + both[m:] + mm(x2[:m], yl, dims)


def kernel(
    near_hbm, leaf_hbm, node_hbm, top_hbm, coords_hbm,
    values_hbm, basis_hbm, ltr_hbm, ntr_hbm, lcp_hbm, ncp_hbm, tcp_hbm,
    out,
    near_ref, leaf_ref, node_ref, top_ref, coords,
    vals, ev, cs, vs, bx, em, en, zb, tb, sm, sn, sc, st,
    basis, ltr, ntr, lcp, ncp, tcp, bh, bl, lth, ltl, nth, ntl, tth, ttl,
    ox, sx, rx,
    local_sem, v_send, v_recv, c_send, c_recv, m_send, m_recv, n_send, n_recv,
    z_send, z_recv, t_send, t_recv, x_send, x_recv, tokens,
):
    leaves, chips = 8, 128
    cols = vals.shape[0]
    d, c = lax.axis_index("leaf"), lax.axis_index("col")
    o = 1 - c
    z, g = lax.rem(d, 8), lax.div(d, 8)
    after, before = lax.rem(d + 1, chips), lax.rem(d + chips - 1, chips)

    def fetch(i, src, dst):
        copy = pltpu.make_async_copy(src, dst, local_sem.at[i])
        copy.start()
        return copy

    get_values = fetch(0, values_hbm, vals)
    quarters = [pl.ds(4 * i, 4) for i in range(2)]
    get_basis = [fetch(1 + i, basis_hbm.at[q], basis.at[q]) for i, q in enumerate(quarters)]
    get_ltr = fetch(3, ltr_hbm, ltr)
    get_ntr = fetch(4, ntr_hbm, ntr)
    get_coords = fetch(5, coords_hbm, coords)
    get_tcp = fetch(6, tcp_hbm.at[g], tcp.at[c])
    get_lists = [
        fetch(7 + i, src, dst)
        for i, (src, dst) in enumerate(
            ((near_hbm, near_ref), (leaf_hbm, leaf_ref), (node_hbm, node_ref), (top_hbm, top_ref))
        )
    ]
    get_lcp = fetch(11, lcp_hbm, lcp)
    get_ncp = fetch(12, ncp_hbm, ncp)

    barrier = pltpu.get_barrier_semaphore()

    def greet(leaf, col):
        pl.semaphore_signal(barrier, inc=1, device_id=(leaf, col), device_id_type=MESH)

    def chip(x, y, z):
        return (lax.rem(x, 4) * 4 + lax.rem(y, 4)) * 8 + lax.rem(z, 8)

    x, y = lax.div(g, 4), lax.rem(g, 4)
    x_up, x_down = chip(x + 1, y, z), chip(x + 3, y, z)
    y_up, y_down = chip(x, y + 1, z), chip(x, y + 3, z)
    z_up, z_down = chip(x, y, z + 1), chip(x, y, z + 7)
    no_after, no_before = lax.div(d, chips - 1), lax.div(chips - 1 - d, chips - 1)
    sides = ((0, after, no_after == 0, no_before == 0), (1, before, no_before == 0, no_after == 0))

    greet(d, o)
    for leaf in (z_up, z_down, x_up, x_down, y_up, y_down):
        greet(leaf, c)
    for _, leaf, there, _ in sides:

        @pl.when(there)
        def _(leaf=leaf):
            greet(leaf, 0)
            greet(leaf, 1)

    def token(i, leaf):
        pl.semaphore_signal(tokens.at[i], inc=1, device_id=(leaf, c), device_id_type=MESH)

    def heard(*which):
        for i in which:
            pl.semaphore_wait(tokens.at[i], 1)

    def remote(src, dst, ssem, rsem, leaf, col):
        return pltpu.make_async_remote_copy(
            src_ref=src, dst_ref=dst, send_sem=ssem, recv_sem=rsem,
            device_id=(leaf, col), device_id_type=MESH,
        )

    sends = []

    def send(*args):
        copy = remote(*args)
        copy.start()
        sends.append(copy)

    own = pl.ds(leaves, leaves)
    zero8 = jnp.zeros((8, 128), F32)

    def points_to(q, leaf):
        land = pl.ds(16 * q, leaves)
        return (
            remote(vals, ev.at[q], v_send.at[q], v_recv.at[q], leaf, c),
            remote(cs.at[own], cs.at[land], c_send.at[q], c_recv.at[q], leaf, c),
        )

    def moments_to(q, leaf):
        land = pl.ds(16 * q, leaves)
        return [
            copy
            for h in range(2)
            for copy in (
                remote(sn.at[h], en.at[c, 2 * q], n_send.at[q, h], n_recv.at[2 * q, c], leaf, h),
                remote(sm.at[h], em.at[c, land], m_send.at[q, h], m_recv.at[2 * q, c], leaf, h),
            )
        ]

    get_coords.wait()
    for l in range(leaves):
        for h in range(2):
            start = l * 256 + h * 128
            cs[leaves + l, 3 * h : 3 * h + 3, :] = coords[:, start : start + 128]
        cs[leaves + l, 6:8, :] = zero8[:2]
    get_values.wait()
    pl.semaphore_wait(barrier, 11 - 2 * no_after - 2 * no_before)
    for q, leaf, there, _ in sides:

        @pl.when(there)
        def _(q=q, leaf=leaf):
            for copy in points_to(q, leaf):
                copy.start()

    token(0, z_up)
    token(3, z_down)
    token(5, x_down)

    for l in range(leaves):
        vs[leaves + l] = stacked(vals[:, l * 256 : (l + 1) * 256])
    moments = []
    for l in range(leaves):
        if l % 4 == 0:
            get_basis[l // 4].wait()
        hi, lo = split(basis[l])
        bh[l], bl[l] = hi, lo
        moments.append(dot3(vs[leaves + l], hi, lo, NN))
    get_ltr.wait()
    lth[...], ltl[...] = split(ltr[...])
    down = (leaves * 128, 128)
    node = dot3(stacked(jnp.concatenate(moments, 1)), lth[...].reshape(down), ltl[...].reshape(down), NN)
    get_ntr.wait()
    nth[...], ntl[...] = split(ntr[0])
    contrib = dot3(stacked(node), nth[...], ntl[...], NN)
    sc[...] = contrib
    heard(0)
    token(1, z_up)
    heard(3)
    token(4, z_down)
    heard(5)
    token(6, y_up)
    token(8, y_down)
    heard(1)
    token(2, z_up)
    heard(4, 2)
    for k in range(1, 8):
        send(sc, zb.at[k], z_send.at[k], z_recv.at[k], g * 8 + lax.rem(z + k, 8), c)

    low = lax.broadcasted_iota(jnp.int32, (8, 128), 1) < 64

    def half(x, h):
        a, b = x[:8], x[8:]
        return jnp.where(low, a, pltpu.roll(b, 64, 1)) if h == 0 else jnp.where(low, pltpu.roll(a, 64, 1), b)

    for h in range(2):
        sn[h] = half(node, h)
        for l in range(leaves):
            sm[h, l] = half(moments[l], h)
    get_tcp.wait()
    send(tcp.at[c], tcp.at[c], x_send.at[1], x_recv.at[1], d, o)
    send(sm.at[o], em.at[c, own], m_send.at[2, o], m_recv.at[1, c], d, o)
    send(sn.at[o], en.at[c, 1], n_send.at[2, o], n_recv.at[1, c], d, o)
    for q, leaf, there, _ in sides:

        @pl.when(there)
        def _(q=q, leaf=leaf):
            for copy in moments_to(q, leaf):
                copy.start()

    em[c, own] = sm[c]
    en[c, 1] = sn[c]

    heard(6)
    token(7, y_up)
    cs[24] = zero8
    vs[24] = jnp.zeros((2 * cols, 256), BF16)
    tb[16] = jnp.zeros((cols, 128), F32)
    for s in range(2):
        em[s, 24] = zero8
        en[s, 3] = zero8

    def source(v, first, none):
        return jnp.where(v >= 0, jnp.clip(v - first, 0, none - 1), none)

    def take_points():
        for q, leaf, _, there in sides:

            @pl.when(there)
            def _(q=q, leaf=leaf):
                for copy in points_to(q, leaf):
                    copy.wait_recv()
                for l in range(leaves):
                    vs[16 * q + l] = stacked(ev[q, :, l * 256 : (l + 1) * 256])

    def near(l, carry):
        points = cs[leaves + l].T
        for k in range(3):
            bx[k, 0:128, :] = jnp.broadcast_to(points[:, k : k + 1], (128, 128))
            bx[k, 128:256, :] = jnp.broadcast_to(points[:, 3 + k : 4 + k], (128, 128))
        total = None
        for j in range(8):
            i = source(near_ref[l, j], (d - 1) * leaves, 24)
            rows = cs[i]
            his, los = [], []
            for h in range(2):
                r2 = None
                for k in range(3):
                    e = bx[k] - rows[3 * h + k : 3 * h + k + 1, :]
                    r2 = e * e if r2 is None else r2 + e * e
                hi, lo = split(lax.rsqrt(r2 + SOFTENING))
                his.append(hi)
                los.append(lo)
            term = dot3(vs[i], jnp.concatenate(his, 1), jnp.concatenate(los, 1), NT)
            total = term if total is None else total + term
        out[:, pl.ds(pl.multiple_of(l * 256, 256), 256)] = total * (1.0 / 16.0)
        return carry

    for copy in get_lists:
        copy.wait()
    ahead = jnp.where(z < 4, AHEAD, 0)

    @pl.when(z < 4)
    def _():
        take_points()

    lax.fori_loop(0, ahead, near, 0)

    total = contrib
    for k in range(1, 8):
        remote(sc, zb.at[k], z_send.at[k], z_recv.at[k], d, o).wait_recv()
    for k in range(1, 8):
        total = total + zb[k]
    st[...] = total
    heard(8, 7)
    for k in range(1, 16):
        send(st, tb.at[g], t_send.at[k], t_recv.at[k], lax.rem(g + k, 16) * 8 + z, c)
    tb[g] = total

    def paired(load, i, j):
        rows = []
        for s in range(2):
            a, b = load(s, i), load(s, j)
            rows += [jnp.where(low, a, pltpu.roll(b, 64, 1)), jnp.where(low, pltpu.roll(a, 64, 1), b)]
        return jnp.concatenate(rows, 0)

    def coupled(load, index, blocks):
        slots = blocks.shape[0]
        picked = jnp.concatenate([paired(load, index(j), index(j + 1)) for j in range(0, slots, 2)], 1)
        return dot3(stacked(picked), *split(blocks.reshape(slots * 64, 128)), NN)

    for q, _, _, there in sides:

        @pl.when(there)
        def _(q=q):
            for h in range(2):
                land = pl.ds(16 * q, leaves)
                remote(sm.at[h], em.at[h, land], m_send.at[0, h], m_recv.at[2 * q, h], d, o).wait_recv()
                remote(sn.at[h], en.at[h, 2 * q], n_send.at[0, h], n_recv.at[2 * q, h], d, o).wait_recv()

    remote(sm.at[o], em.at[o, own], m_send.at[2, o], m_recv.at[1, o], d, o).wait_recv()
    remote(sn.at[o], en.at[o, 1], n_send.at[2, o], n_recv.at[1, o], d, o).wait_recv()
    for copy in (get_lcp, get_ncp):
        copy.wait()
    first = jnp.full((cols, 128), c, jnp.int32) == 0

    def keep(i, both):
        a, b = both[:cols], both[cols:]
        ox[i] = jnp.where(first, a, b)
        sx[i] = jnp.where(first, b, a)

    for l in range(leaves):
        keep(l, coupled(lambda s, i: em[s, i], lambda j: source(leaf_ref[l, j], (d - 1) * leaves, 24), lcp[l]))
    keep(leaves, coupled(lambda s, i: en[s, i], lambda j: source(node_ref[0, j], d - 1, 3), ncp[0]))
    send(sx, rx, x_send.at[0], x_recv.at[0], d, o)
    remote(tcp.at[o], tcp.at[o], x_send.at[1], x_recv.at[1], d, o).wait_recv()
    for j in range(4):
        for h in range(2):
            rows = pl.ds(j * 128 + h * 64, 64)
            tth[rows], ttl[rows] = split(tcp[h, j])

    @pl.when(z >= 4)
    def _():
        take_points()

    lax.fori_loop(ahead, 8, near, 0)

    remote(sx, rx, x_send.at[0], x_recv.at[0], d, o).wait_recv()
    for k in range(1, 16):
        remote(st, tb.at[g], t_send.at[k], t_recv.at[k], d, o).wait_recv()
    picked = jnp.concatenate([tb[source(top_ref[j, g], 0, 16)] for j in range(4)], 1)
    top_local = dot3(stacked(picked), tth[...], ttl[...], NN)
    node_local = ox[leaves] + rx[leaves] + dot3(stacked(top_local), nth[...], ntl[...], NT)
    node2 = stacked(node_local)
    for l in range(leaves):
        leaf_local = ox[l] + rx[l] + dot3(node2, lth[l], ltl[l], NT)
        far = dot3(stacked(leaf_local), bh[l], bl[l], NT)
        out[:, l * 256 : (l + 1) * 256] = out[:, l * 256 : (l + 1) * 256] + far
    for copy in sends:
        copy.wait_send()
    for q, leaf, there, _ in sides:

        @pl.when(there)
        def _(q=q, leaf=leaf):
            for copy in (*points_to(q, leaf), *moments_to(q, leaf)):
                copy.wait_send()


def body(
    coords, values, leaf_basis, leaf_transfer, node_transfer, leaf_coupling, node_coupling, top_coupling,
    near_list, leaf_list, node_list, top_list,
):
    cols = values.shape[0]
    any_ref = pl.BlockSpec(memory_space=pl.ANY)
    vmem = pl.BlockSpec(memory_space=pltpu.VMEM)
    dma = pltpu.SemaphoreType.DMA
    return pl.pallas_call(
        kernel,
        out_shape=jax.ShapeDtypeStruct(values.shape, F32),
        in_specs=[any_ref] * 12,
        out_specs=vmem,
        scratch_shapes=[
            pltpu.SMEM((8, 8), jnp.int32),
            pltpu.SMEM((8, 8), jnp.int32),
            pltpu.SMEM((1, 2), jnp.int32),
            pltpu.SMEM((4, 16), jnp.int32),
            pltpu.VMEM((3, 2048), F32),
            pltpu.VMEM((cols, 2048), F32),
            pltpu.VMEM((2, cols, 2048), F32),
            pltpu.VMEM((25, 8, 128), F32),
            pltpu.VMEM((25, 2 * cols, 256), BF16),
            pltpu.VMEM((3, 256, 128), F32),
            pltpu.VMEM((2, 25, 8, 128), F32),
            pltpu.VMEM((2, 4, 8, 128), F32),
            pltpu.VMEM((8, cols, 128), F32),
            pltpu.VMEM((17, cols, 128), F32),
            pltpu.VMEM((2, 8, 8, 128), F32),
            pltpu.VMEM((2, 8, 128), F32),
            pltpu.VMEM((cols, 128), F32),
            pltpu.VMEM((cols, 128), F32),
            pltpu.VMEM((8, 256, 128), F32),
            pltpu.VMEM((8, 128, 128), F32),
            pltpu.VMEM((1, 128, 128), F32),
            pltpu.VMEM((8, 8, 64, 128), F32),
            pltpu.VMEM((1, 2, 64, 128), F32),
            pltpu.VMEM((2, 4, 64, 128), F32),
            pltpu.VMEM((8, 256, 128), BF16),
            pltpu.VMEM((8, 256, 128), BF16),
            pltpu.VMEM((8, 128, 128), BF16),
            pltpu.VMEM((8, 128, 128), BF16),
            pltpu.VMEM((128, 128), BF16),
            pltpu.VMEM((128, 128), BF16),
            pltpu.VMEM((512, 128), BF16),
            pltpu.VMEM((512, 128), BF16),
            pltpu.VMEM((9, cols, 128), F32),
            pltpu.VMEM((9, cols, 128), F32),
            pltpu.VMEM((9, cols, 128), F32),
            dma((13,)),
            dma((2,)), dma((2,)), dma((2,)), dma((2,)),
            dma((3, 2)), dma((3, 2)), dma((3, 2)), dma((3, 2)),
            dma((8,)), dma((8,)), dma((16,)), dma((16,)),
            dma((2,)), dma((2,)), pltpu.SemaphoreType.REGULAR((9,)),
        ],
        compiler_params=pltpu.CompilerParams(collective_id=0, has_side_effects=True),
    )(
        near_list, leaf_list, node_list, top_list.T, coords, values,
        leaf_basis, leaf_transfer, node_transfer, leaf_coupling, node_coupling, top_coupling,
    )


def solution(mesh):
    in_specs = (
        P(None, "leaf"),
        P("col", "leaf"),
        P("leaf", None, None),
        P("leaf", None, None),
        P("leaf", None, None),
        P("leaf", None, "col", None),
        P("leaf", None, "col", None),
        P(None, None, "col", None),
        P("leaf", None),
        P("leaf", None),
        P("leaf", None),
        P(),
    )
    return jax.shard_map(body, mesh=mesh, in_specs=in_specs, out_specs=P("col", "leaf"), check_vma=False)
```

```python
import functools

import jax
import jax.numpy as jnp
from jax import lax
from jax.experimental import pallas as pl
from jax.experimental.pallas import tpu as pltpu
from jax.sharding import PartitionSpec as P

SOFTENING = 0.01
F32, BF16 = jnp.float32, jnp.bfloat16
MESH = pl.DeviceIdType.MESH
NN = (((1,), (0,)), ((), ()))
NT = (((1,), (1,)), ((), ()))


def mm(a, b, dims):
    return lax.dot_general(a, b, dims, preferred_element_type=F32)


def split(x):
    hi = x.astype(BF16)
    return hi, (x - hi.astype(F32)).astype(BF16)


def stacked(x):
    return jnp.concatenate(split(x), axis=0)


def dot3(x2, yh, yl, dims):
    m = x2.shape[0] // 2
    both = mm(x2, yh, dims)
    return both[:m] + both[m:] + mm(x2[:m], yl, dims)


def kernel(
    near_hbm, leaf_hbm, node_hbm, top_hbm, coords_hbm,
    values_hbm, basis_hbm, ltr_hbm, ntr_hbm, lcp_hbm, ncp_hbm, tcp_hbm,
    out,
    near_ref, leaf_ref, node_ref, top_ref, coords,
    vals, ev, cs, rv, vs, nk, ns, nr, bx, em, en, zb, tb, sm, sn, sc, st,
    basis, ltr, ntr, lcp, ncp, tcp, bh, bl, lth, ltl, nth, ntl, tth, ttl,
    ox, sx, rx,
    local_sem, v_send, v_recv, c_send, c_recv, m_send, m_recv, n_send, n_recv,
    z_send, z_recv, t_send, t_recv, x_send, x_recv, f_send, f_recv, g_send, g_recv, r_send, r_recv, tokens,
):
    leaves, chips = 8, 128
    cols = vals.shape[0]
    d, c = lax.axis_index("leaf"), lax.axis_index("col")
    o = 1 - c
    z, g = lax.rem(d, 8), lax.div(d, 8)
    after, before = lax.rem(d + 1, chips), lax.rem(d + chips - 1, chips)

    def fetch(i, src, dst):
        copy = pltpu.make_async_copy(src, dst, local_sem.at[i])
        copy.start()
        return copy

    get_values = fetch(0, values_hbm, vals)
    quarters = [pl.ds(4 * i, 4) for i in range(2)]
    get_basis = [fetch(1 + i, basis_hbm.at[q], basis.at[q]) for i, q in enumerate(quarters)]
    get_ltr = fetch(3, ltr_hbm, ltr)
    get_ntr = fetch(4, ntr_hbm, ntr)
    get_coords = fetch(5, coords_hbm, coords)
    get_tcp = fetch(6, tcp_hbm.at[g], tcp.at[c])
    get_lists = [
        fetch(7 + i, src, dst)
        for i, (src, dst) in enumerate(
            ((near_hbm, near_ref), (leaf_hbm, leaf_ref), (node_hbm, node_ref), (top_hbm, top_ref))
        )
    ]
    get_lcp = fetch(11, lcp_hbm, lcp)
    get_ncp = fetch(12, ncp_hbm, ncp)

    barrier = pltpu.get_barrier_semaphore()

    def greet(leaf, col):
        pl.semaphore_signal(barrier, inc=1, device_id=(leaf, col), device_id_type=MESH)

    def chip(x, y, z):
        return (lax.rem(x, 4) * 4 + lax.rem(y, 4)) * 8 + lax.rem(z, 8)

    x, y = lax.div(g, 4), lax.rem(g, 4)
    x_up, x_down = chip(x + 1, y, z), chip(x + 3, y, z)
    y_up, y_down = chip(x, y + 1, z), chip(x, y + 3, z)
    z_up, z_down = chip(x, y, z + 1), chip(x, y, z + 7)
    no_after, no_before = lax.div(d, chips - 1), lax.div(chips - 1 - d, chips - 1)
    sides = ((0, after, no_after == 0, no_before == 0), (1, before, no_before == 0, no_after == 0))

    greet(d, o)
    for leaf in (z_up, z_down, x_up, x_down, y_up, y_down):
        greet(leaf, c)
    for _, leaf, there, _ in sides:

        @pl.when(there)
        def _(leaf=leaf):
            greet(leaf, 0)
            greet(leaf, 1)

    def token(i, leaf):
        pl.semaphore_signal(tokens.at[i], inc=1, device_id=(leaf, c), device_id_type=MESH)

    def heard(*which):
        for i in which:
            pl.semaphore_wait(tokens.at[i], 1)

    def remote(src, dst, ssem, rsem, leaf, col):
        return pltpu.make_async_remote_copy(
            src_ref=src, dst_ref=dst, send_sem=ssem, recv_sem=rsem,
            device_id=(leaf, col), device_id_type=MESH,
        )

    sends = []

    def send(*args):
        copy = remote(*args)
        copy.start()
        sends.append(copy)

    own = pl.ds(leaves, leaves)
    zero8 = jnp.zeros((8, 128), F32)

    def columns_to(q, leaf, part):
        rows = pl.ds(part * 8, 8)
        return remote(vals.at[rows], ev.at[q, rows], v_send.at[q, part], v_recv.at[q, part], leaf, c)

    def coords_to(q, leaf):
        mine, land = pl.ds(leaves + 4 * c, 4), pl.ds(16 * q + 4 * c, 4)
        return remote(cs.at[mine], cs.at[land], c_send.at[q], c_recv.at[q], leaf, c)

    def moments_to(q, leaf):
        land = pl.ds(16 * q, leaves)
        return [
            copy
            for h in range(2)
            for copy in (
                remote(sn.at[h], en.at[c, 2 * q], n_send.at[q, h], n_recv.at[2 * q, c], leaf, h),
                remote(sm.at[h], em.at[c, land], m_send.at[q, h], m_recv.at[2 * q, c], leaf, h),
            )
        ]

    get_coords.wait()
    for l in range(leaves):
        for h in range(2):
            start = l * 256 + h * 128
            cs[leaves + l, 3 * h : 3 * h + 3, :] = coords[:, start : start + 128]
        cs[leaves + l, 6:8, :] = zero8[:2]
    get_values.wait()
    pl.semaphore_wait(barrier, 11 - 2 * no_after - 2 * no_before)
    for q, leaf, there, _ in sides:

        @pl.when(there)
        def _(q=q, leaf=leaf):
            coords_to(q, leaf).start()
            columns_to(q, leaf, 0).start()
            columns_to(q, leaf, 1).start()

    send(vals, rv.at[2], f_send.at[2], f_recv.at[2], d, o)
    token(0, z_up)
    token(3, z_down)
    token(5, x_down)

    for l in range(leaves):
        vs[c, leaves + l] = stacked(vals[:, l * 256 : (l + 1) * 256])
    moments = []
    for l in range(leaves):
        if l % 4 == 0:
            get_basis[l // 4].wait()
        hi, lo = split(basis[l])
        bh[l], bl[l] = hi, lo
        moments.append(dot3(vs[c, leaves + l], hi, lo, NN))
    get_ltr.wait()
    lth[...], ltl[...] = split(ltr[...])
    down = (leaves * 128, 128)
    node = dot3(stacked(jnp.concatenate(moments, 1)), lth[...].reshape(down), ltl[...].reshape(down), NN)
    get_ntr.wait()
    nth[...], ntl[...] = split(ntr[0])
    contrib = dot3(stacked(node), nth[...], ntl[...], NN)
    sc[...] = contrib
    heard(0)
    token(1, z_up)
    heard(3)
    token(4, z_down)
    heard(5)
    token(6, y_up)
    token(8, y_down)
    heard(1)
    token(2, z_up)
    heard(4, 2)
    for k in range(1, 8):
        send(sc, zb.at[k], z_send.at[k], z_recv.at[k], g * 8 + lax.rem(z + k, 8), c)

    low = lax.broadcasted_iota(jnp.int32, (8, 128), 1) < 64

    def half(x, h):
        a, b = x[:8], x[8:]
        return jnp.where(low, a, pltpu.roll(b, 64, 1)) if h == 0 else jnp.where(low, pltpu.roll(a, 64, 1), b)

    for h in range(2):
        sn[h] = half(node, h)
        for l in range(leaves):
            sm[h, l] = half(moments[l], h)
    get_tcp.wait()
    send(tcp.at[c], tcp.at[c], x_send.at[1], x_recv.at[1], d, o)
    send(sm.at[o], em.at[c, own], m_send.at[2, o], m_recv.at[1, c], d, o)
    send(sn.at[o], en.at[c, 1], n_send.at[2, o], n_recv.at[1, c], d, o)
    for q, leaf, there, _ in sides:

        @pl.when(there)
        def _(q=q, leaf=leaf):
            for copy in moments_to(q, leaf):
                copy.start()

    em[c, own] = sm[c]
    en[c, 1] = sn[c]

    heard(6)
    token(7, y_up)
    cs[24] = zero8
    tb[16] = jnp.zeros((cols, 128), F32)
    for s in range(2):
        vs[s, 24] = jnp.zeros((2 * cols, 256), BF16)
        em[s, 24] = zero8
        en[s, 3] = zero8

    def source(v, first, none):
        return jnp.where(v >= 0, jnp.clip(v - first, 0, none - 1), none)

    def forward(q):
        return remote(ev.at[q], rv.at[q], f_send.at[q], f_recv.at[q], d, o)

    def forward_coords(q, core):
        land = cs.at[pl.ds(16 * q + 4 * core, 4)]
        return remote(land, land, g_send.at[q], g_recv.at[q], d, o)

    def pass_on():
        for q, leaf, _, there in sides:

            @pl.when(there)
            def _(q=q, leaf=leaf):
                coords_to(q, leaf).wait_recv()
                forward_coords(q, c).start()
                for part in range(2):
                    columns_to(q, leaf, part).wait_recv()
                forward(q).start()

    def take_points():
        for q, _, _, there in sides:

            @pl.when(there)
            def _(q=q):
                for l in range(leaves):
                    vs[c, 16 * q + l] = stacked(ev[q, :, l * 256 : (l + 1) * 256])

        remote(vals, rv.at[2], f_send.at[2], f_recv.at[2], d, o).wait_recv()
        for l in range(leaves):
            vs[o, leaves + l] = stacked(rv[2, :, l * 256 : (l + 1) * 256])
        for q, _, _, there in sides:

            @pl.when(there)
            def _(q=q):
                forward_coords(q, o).wait_recv()
                forward(q).wait_recv()
                for l in range(leaves):
                    vs[o, 16 * q + l] = stacked(rv[q, :, l * 256 : (l + 1) * 256])

    first = jnp.full((cols, 128), c, jnp.int32) == 0
    wide = jnp.full((cols, 256), c, jnp.int32) == 0

    def result(t):
        return remote(ns.at[t], nr.at[t], r_send.at[t], r_recv.at[t], d, o)

    def near(t, carry):
        l = c * 4 + t
        points = cs[leaves + l].T
        for k in range(3):
            bx[k, 0:128, :] = jnp.broadcast_to(points[:, k : k + 1], (128, 128))
            bx[k, 128:256, :] = jnp.broadcast_to(points[:, 3 + k : 4 + k], (128, 128))
        total = None
        for j in range(8):
            i = source(near_ref[l, j], (d - 1) * leaves, 24)
            rows = cs[i]
            his, los = [], []
            for h in range(2):
                r2 = None
                for k in range(3):
                    e = bx[k] - rows[3 * h + k : 3 * h + k + 1, :]
                    r2 = e * e if r2 is None else r2 + e * e
                hi, lo = split(lax.rsqrt(r2 + SOFTENING))
                his.append(hi)
                los.append(lo)
            v0, v1 = vs[0, i], vs[1, i]
            v2 = jnp.concatenate([v0[:cols], v1[:cols], v0[cols:], v1[cols:]], 0)
            term = dot3(v2, jnp.concatenate(his, 1), jnp.concatenate(los, 1), NT)
            total = term if total is None else total + term
        total = total * (1.0 / 16.0)
        a, b = total[:cols], total[cols:]
        nk[t] = jnp.where(wide, a, b)
        ns[t] = jnp.where(wide, b, a)
        result(t).start()
        return carry

    for copy in get_lists:
        copy.wait()
    pass_on()
    total = contrib
    for k in range(1, 8):
        remote(sc, zb.at[k], z_send.at[k], z_recv.at[k], d, o).wait_recv()
    for k in range(1, 8):
        total = total + zb[k]
    st[...] = total
    heard(8, 7)
    for k in range(1, 16):
        send(st, tb.at[g], t_send.at[k], t_recv.at[k], lax.rem(g + k, 16) * 8 + z, c)
    tb[g] = total

    def paired(load, i, j):
        rows = []
        for s in range(2):
            a, b = load(s, i), load(s, j)
            rows += [jnp.where(low, a, pltpu.roll(b, 64, 1)), jnp.where(low, pltpu.roll(a, 64, 1), b)]
        return jnp.concatenate(rows, 0)

    def coupled(load, index, blocks):
        slots = blocks.shape[0]
        picked = jnp.concatenate([paired(load, index(j), index(j + 1)) for j in range(0, slots, 2)], 1)
        return dot3(stacked(picked), *split(blocks.reshape(slots * 64, 128)), NN)

    for q, _, _, there in sides:

        @pl.when(there)
        def _(q=q):
            for h in range(2):
                land = pl.ds(16 * q, leaves)
                remote(sm.at[h], em.at[h, land], m_send.at[0, h], m_recv.at[2 * q, h], d, o).wait_recv()
                remote(sn.at[h], en.at[h, 2 * q], n_send.at[0, h], n_recv.at[2 * q, h], d, o).wait_recv()

    remote(sm.at[o], em.at[o, own], m_send.at[2, o], m_recv.at[1, o], d, o).wait_recv()
    remote(sn.at[o], en.at[o, 1], n_send.at[2, o], n_recv.at[1, o], d, o).wait_recv()
    for copy in (get_lcp, get_ncp):
        copy.wait()

    def keep(i, both):
        a, b = both[:cols], both[cols:]
        ox[i] = jnp.where(first, a, b)
        sx[i] = jnp.where(first, b, a)

    for l in range(leaves):
        keep(l, coupled(lambda s, i: em[s, i], lambda j: source(leaf_ref[l, j], (d - 1) * leaves, 24), lcp[l]))
    keep(leaves, coupled(lambda s, i: en[s, i], lambda j: source(node_ref[0, j], d - 1, 3), ncp[0]))
    send(sx, rx, x_send.at[0], x_recv.at[0], d, o)
    remote(tcp.at[o], tcp.at[o], x_send.at[1], x_recv.at[1], d, o).wait_recv()
    for j in range(4):
        for h in range(2):
            rows = pl.ds(j * 128 + h * 64, 64)
            tth[rows], ttl[rows] = split(tcp[h, j])

    take_points()
    lax.fori_loop(0, 4, near, 0)

    remote(sx, rx, x_send.at[0], x_recv.at[0], d, o).wait_recv()
    for k in range(1, 16):
        remote(st, tb.at[g], t_send.at[k], t_recv.at[k], d, o).wait_recv()
    picked = jnp.concatenate([tb[source(top_ref[j, g], 0, 16)] for j in range(4)], 1)
    top_local = dot3(stacked(picked), tth[...], ttl[...], NN)
    node_local = ox[leaves] + rx[leaves] + dot3(stacked(top_local), nth[...], ntl[...], NT)
    node2 = stacked(node_local)
    for l in range(leaves):
        leaf_local = ox[l] + rx[l] + dot3(node2, lth[l], ltl[l], NT)
        far = dot3(stacked(leaf_local), bh[l], bl[l], NT)
        out[:, l * 256 : (l + 1) * 256] = far
    for t in range(4):
        result(t).wait_recv()
    for l in range(leaves):
        t, span = l % 4, slice(l * 256, (l + 1) * 256)
        close = jnp.where(wide, nk[t], nr[t]) if l < 4 else jnp.where(wide, nr[t], nk[t])
        out[:, span] = out[:, span] + close
    for copy in sends:
        copy.wait_send()
    for q, leaf, there, _ in sides:

        @pl.when(there)
        def _(q=q, leaf=leaf):
            points = [coords_to(q, leaf), columns_to(q, leaf, 0), columns_to(q, leaf, 1)]
            for copy in (*points, *moments_to(q, leaf)):
                copy.wait_send()

    for q, _, _, there in sides:

        @pl.when(there)
        def _(q=q):
            forward(q).wait_send()
            forward_coords(q, c).wait_send()

    for t in range(4):
        result(t).wait_send()


def body(
    coords, values, leaf_basis, leaf_transfer, node_transfer, leaf_coupling, node_coupling, top_coupling,
    near_list, leaf_list, node_list, top_list,
):
    cols = values.shape[0]
    any_ref = pl.BlockSpec(memory_space=pl.ANY)
    vmem = pl.BlockSpec(memory_space=pltpu.VMEM)
    dma = pltpu.SemaphoreType.DMA
    return pl.pallas_call(
        kernel,
        out_shape=pltpu.VMEM(values.shape, F32),
        in_specs=[any_ref] * 12,
        out_specs=vmem,
        scratch_shapes=[
            pltpu.SMEM((8, 8), jnp.int32),
            pltpu.SMEM((8, 8), jnp.int32),
            pltpu.SMEM((1, 2), jnp.int32),
            pltpu.SMEM((4, 16), jnp.int32),
            pltpu.VMEM((3, 2048), F32),
            pltpu.VMEM((cols, 2048), F32),
            pltpu.VMEM((2, cols, 2048), F32),
            pltpu.VMEM((25, 8, 128), F32),
            pltpu.VMEM((3, cols, 2048), F32),
            pltpu.VMEM((2, 25, 2 * cols, 256), BF16),
            pltpu.VMEM((4, cols, 256), F32),
            pltpu.VMEM((4, cols, 256), F32),
            pltpu.VMEM((4, cols, 256), F32),
            pltpu.VMEM((3, 256, 128), F32),
            pltpu.VMEM((2, 25, 8, 128), F32),
            pltpu.VMEM((2, 4, 8, 128), F32),
            pltpu.VMEM((8, cols, 128), F32),
            pltpu.VMEM((17, cols, 128), F32),
            pltpu.VMEM((2, 8, 8, 128), F32),
            pltpu.VMEM((2, 8, 128), F32),
            pltpu.VMEM((cols, 128), F32),
            pltpu.VMEM((cols, 128), F32),
            pltpu.VMEM((8, 256, 128), F32),
            pltpu.VMEM((8, 128, 128), F32),
            pltpu.VMEM((1, 128, 128), F32),
            pltpu.VMEM((8, 8, 64, 128), F32),
            pltpu.VMEM((1, 2, 64, 128), F32),
            pltpu.VMEM((2, 4, 64, 128), F32),
            pltpu.VMEM((8, 256, 128), BF16),
            pltpu.VMEM((8, 256, 128), BF16),
            pltpu.VMEM((8, 128, 128), BF16),
            pltpu.VMEM((8, 128, 128), BF16),
            pltpu.VMEM((128, 128), BF16),
            pltpu.VMEM((128, 128), BF16),
            pltpu.VMEM((512, 128), BF16),
            pltpu.VMEM((512, 128), BF16),
            pltpu.VMEM((9, cols, 128), F32),
            pltpu.VMEM((9, cols, 128), F32),
            pltpu.VMEM((9, cols, 128), F32),
            dma((13,)),
            dma((2, 2)), dma((2, 2)), dma((2,)), dma((2,)),
            dma((3, 2)), dma((3, 2)), dma((3, 2)), dma((3, 2)),
            dma((8,)), dma((8,)), dma((16,)), dma((16,)),
            dma((2,)), dma((2,)), dma((3,)), dma((3,)), dma((2,)), dma((2,)), dma((4,)), dma((4,)), pltpu.SemaphoreType.REGULAR((9,)),
        ],
        compiler_params=pltpu.CompilerParams(collective_id=0, has_side_effects=True),
    )(
        near_list, leaf_list, node_list, top_list.T, coords, values,
        leaf_basis, leaf_transfer, node_transfer, leaf_coupling, node_coupling, top_coupling,
    )


def solution(mesh):
    in_specs = (
        P(None, "leaf"),
        P("col", "leaf"),
        P("leaf", None, None),
        P("leaf", None, None),
        P("leaf", None, None),
        P("leaf", None, "col", None),
        P("leaf", None, "col", None),
        P(None, None, "col", None),
        P("leaf", None),
        P("leaf", None),
        P("leaf", None),
        P(),
    )
    return jax.shard_map(body, mesh=mesh, in_specs=in_specs, out_specs=P("col", "leaf"), check_vma=False)
```

```python
import functools

import jax
import jax.numpy as jnp
from jax import lax
from jax.experimental import pallas as pl
from jax.experimental.pallas import tpu as pltpu
from jax.sharding import PartitionSpec as P

SOFTENING = 0.01
F32, BF16 = jnp.float32, jnp.bfloat16
MESH = pl.DeviceIdType.MESH
NN = (((1,), (0,)), ((), ()))
NT = (((1,), (1,)), ((), ()))


def mm(a, b, dims):
    return lax.dot_general(a, b, dims, preferred_element_type=F32)


def split(x):
    hi = x.astype(BF16)
    return hi, (x - hi.astype(F32)).astype(BF16)


def stacked(x):
    return jnp.concatenate(split(x), axis=0)


def dot3(x2, yh, yl, dims):
    m = x2.shape[0] // 2
    both = mm(x2, yh, dims)
    return both[:m] + both[m:] + mm(x2[:m], yl, dims)


def kernel(
    near_hbm, leaf_hbm, node_hbm, top_hbm, coords_hbm,
    values_hbm, basis_hbm, ltr_hbm, ntr_hbm, lcp_hbm, ncp_hbm, tcp_hbm,
    out,
    near_ref, leaf_ref, node_ref, top_ref, coords,
    vals, ev, cs, rv, vs, nk, ns, nr, bx, em, en, zb, tb, sm, sn, sc, st,
    basis, ltr, ntr, lcp, ncp, tcp, bh, bl, lth, ltl, nth, ntl, tth, ttl,
    ox, sx, rx,
    local_sem, v_send, v_recv, c_send, c_recv, m_send, m_recv, n_send, n_recv,
    z_send, z_recv, t_send, t_recv, x_send, x_recv, f_send, f_recv, g_send, g_recv, r_send, r_recv, tokens, answers,
):
    leaves, chips = 8, 128
    cols = vals.shape[0]
    d, c = lax.axis_index("leaf"), lax.axis_index("col")
    o = 1 - c
    z, g = lax.rem(d, 8), lax.div(d, 8)
    after, before = lax.rem(d + 1, chips), lax.rem(d + chips - 1, chips)

    def fetch(i, src, dst):
        copy = pltpu.make_async_copy(src, dst, local_sem.at[i])
        copy.start()
        return copy

    get_values = fetch(0, values_hbm, vals)
    quarters = [pl.ds(4 * i, 4) for i in range(2)]
    get_basis = [fetch(1 + i, basis_hbm.at[q], basis.at[q]) for i, q in enumerate(quarters)]
    get_ltr = fetch(3, ltr_hbm, ltr)
    get_ntr = fetch(4, ntr_hbm, ntr)
    get_coords = fetch(5, coords_hbm, coords)
    get_tcp = fetch(6, tcp_hbm.at[g], tcp.at[c])
    get_lists = [
        fetch(7 + i, src, dst)
        for i, (src, dst) in enumerate(
            ((near_hbm, near_ref), (leaf_hbm, leaf_ref), (node_hbm, node_ref), (top_hbm, top_ref))
        )
    ]
    get_lcp = fetch(11, lcp_hbm, lcp)
    get_ncp = fetch(12, ncp_hbm, ncp)

    barrier = pltpu.get_barrier_semaphore()

    def greet(leaf, col):
        pl.semaphore_signal(barrier, inc=1, device_id=(leaf, col), device_id_type=MESH)

    def chip(x, y, z):
        return (lax.rem(x, 4) * 4 + lax.rem(y, 4)) * 8 + lax.rem(z, 8)

    x, y = lax.div(g, 4), lax.rem(g, 4)
    x_up, x_down = chip(x + 1, y, z), chip(x + 3, y, z)
    y_up, y_down = chip(x, y + 1, z), chip(x, y + 3, z)
    z_up, z_down = chip(x, y, z + 1), chip(x, y, z + 7)
    no_after, no_before = lax.div(d, chips - 1), lax.div(chips - 1 - d, chips - 1)
    sides = ((0, after, no_after == 0, no_before == 0), (1, before, no_before == 0, no_after == 0))

    greet(d, o)
    greet(z_up, c)
    greet(z_down, c)
    for _, leaf, there, _ in sides:

        @pl.when(there)
        def _(leaf=leaf):
            greet(leaf, 0)
            greet(leaf, 1)

    def relation(mine, theirs, leaf, farther):
        return mine, theirs, leaf, farther, jnp.logical_not(farther)

    relations = (
        relation(0, 1, x_up, x < 3),
        relation(1, 0, x_down, x == 0),
        relation(2, 3, y_up, y < 3),
        relation(3, 2, y_down, y == 0),
    )
    for _, _, leaf, far, _ in relations:

        @pl.when(far)
        def _(leaf=leaf):
            greet(leaf, c)

    greeters = sum(near.astype(jnp.int32) for *_, near in relations)

    def answer():
        for _, theirs, leaf, _, near in relations:

            @pl.when(near)
            def _(theirs=theirs, leaf=leaf):
                pl.semaphore_signal(answers.at[theirs], inc=1, device_id=(leaf, c), device_id_type=MESH)

    def known():
        for mine, _, _, far, _ in relations:

            @pl.when(far)
            def _(mine=mine):
                pl.semaphore_wait(answers.at[mine], 1)

    def token(i, leaf):
        pl.semaphore_signal(tokens.at[i], inc=1, device_id=(leaf, c), device_id_type=MESH)

    def heard(*which):
        for i in which:
            pl.semaphore_wait(tokens.at[i], 1)

    def remote(src, dst, ssem, rsem, leaf, col):
        return pltpu.make_async_remote_copy(
            src_ref=src, dst_ref=dst, send_sem=ssem, recv_sem=rsem,
            device_id=(leaf, col), device_id_type=MESH,
        )

    sends = []

    def send(*args):
        copy = remote(*args)
        copy.start()
        sends.append(copy)

    own = pl.ds(leaves, leaves)
    zero8 = jnp.zeros((8, 128), F32)

    def columns_to(q, leaf, part):
        rows = pl.ds(part * 8, 8)
        return remote(vals.at[rows], ev.at[q, rows], v_send.at[q, part], v_recv.at[q, part], leaf, c)

    def coords_to(q, leaf):
        mine, land = pl.ds(leaves + 4 * c, 4), pl.ds(16 * q + 4 * c, 4)
        return remote(cs.at[mine], cs.at[land], c_send.at[q], c_recv.at[q], leaf, c)

    def moments_to(q, leaf):
        land = pl.ds(16 * q, leaves)
        return [
            copy
            for h in range(2)
            for copy in (
                remote(sn.at[h], en.at[c, 2 * q], n_send.at[q, h], n_recv.at[2 * q, c], leaf, h),
                remote(sm.at[h], em.at[c, land], m_send.at[q, h], m_recv.at[2 * q, c], leaf, h),
            )
        ]

    get_coords.wait()
    for l in range(leaves):
        for h in range(2):
            start = l * 256 + h * 128
            cs[leaves + l, 3 * h : 3 * h + 3, :] = coords[:, start : start + 128]
        cs[leaves + l, 6:8, :] = zero8[:2]
    get_values.wait()
    pl.semaphore_wait(barrier, 7 - 2 * no_after - 2 * no_before + greeters)
    for q, leaf, there, _ in sides:

        @pl.when(there)
        def _(q=q, leaf=leaf):
            coords_to(q, leaf).start()
            columns_to(q, leaf, 0).start()
            columns_to(q, leaf, 1).start()

    send(vals, rv.at[2], f_send.at[2], f_recv.at[2], d, o)
    token(0, z_up)
    token(3, z_down)
    answer()

    for l in range(leaves):
        vs[c, leaves + l] = stacked(vals[:, l * 256 : (l + 1) * 256])
    moments = []
    for l in range(leaves):
        if l % 4 == 0:
            get_basis[l // 4].wait()
        hi, lo = split(basis[l])
        bh[l], bl[l] = hi, lo
        moments.append(dot3(vs[c, leaves + l], hi, lo, NN))
    get_ltr.wait()
    lth[...], ltl[...] = split(ltr[...])
    down = (leaves * 128, 128)
    node = dot3(stacked(jnp.concatenate(moments, 1)), lth[...].reshape(down), ltl[...].reshape(down), NN)
    get_ntr.wait()
    nth[...], ntl[...] = split(ntr[0])
    contrib = dot3(stacked(node), nth[...], ntl[...], NN)
    sc[...] = contrib
    heard(0)
    token(1, z_up)
    heard(3)
    token(4, z_down)
    heard(1)
    token(2, z_up)
    heard(4, 2)
    for k in range(1, 8):
        send(sc, zb.at[k], z_send.at[k], z_recv.at[k], g * 8 + lax.rem(z + k, 8), c)

    low = lax.broadcasted_iota(jnp.int32, (8, 128), 1) < 64

    def half(x, h):
        a, b = x[:8], x[8:]
        return jnp.where(low, a, pltpu.roll(b, 64, 1)) if h == 0 else jnp.where(low, pltpu.roll(a, 64, 1), b)

    known()
    token(5, x_down)
    for h in range(2):
        sn[h] = half(node, h)
        for l in range(leaves):
            sm[h, l] = half(moments[l], h)
    get_tcp.wait()
    send(tcp.at[c], tcp.at[c], x_send.at[1], x_recv.at[1], d, o)
    send(sm.at[o], em.at[c, own], m_send.at[2, o], m_recv.at[1, c], d, o)
    send(sn.at[o], en.at[c, 1], n_send.at[2, o], n_recv.at[1, c], d, o)
    for q, leaf, there, _ in sides:

        @pl.when(there)
        def _(q=q, leaf=leaf):
            for copy in moments_to(q, leaf):
                copy.start()

    em[c, own] = sm[c]
    en[c, 1] = sn[c]

    heard(5)
    token(6, y_up)
    token(8, y_down)
    heard(6)
    token(7, y_up)
    cs[24] = zero8
    tb[16] = jnp.zeros((cols, 128), F32)
    for s in range(2):
        vs[s, 24] = jnp.zeros((2 * cols, 256), BF16)
        em[s, 24] = zero8
        en[s, 3] = zero8

    def source(v, first, none):
        return jnp.where(v >= 0, jnp.clip(v - first, 0, none - 1), none)

    def forward(q):
        return remote(ev.at[q], rv.at[q], f_send.at[q], f_recv.at[q], d, o)

    def forward_coords(q, core):
        land = cs.at[pl.ds(16 * q + 4 * core, 4)]
        return remote(land, land, g_send.at[q], g_recv.at[q], d, o)

    def pass_on():
        for q, leaf, _, there in sides:

            @pl.when(there)
            def _(q=q, leaf=leaf):
                coords_to(q, leaf).wait_recv()
                forward_coords(q, c).start()
                for part in range(2):
                    columns_to(q, leaf, part).wait_recv()
                forward(q).start()

    def take_points():
        for q, _, _, there in sides:

            @pl.when(there)
            def _(q=q):
                for l in range(leaves):
                    vs[c, 16 * q + l] = stacked(ev[q, :, l * 256 : (l + 1) * 256])

        remote(vals, rv.at[2], f_send.at[2], f_recv.at[2], d, o).wait_recv()
        for l in range(leaves):
            vs[o, leaves + l] = stacked(rv[2, :, l * 256 : (l + 1) * 256])
        for q, _, _, there in sides:

            @pl.when(there)
            def _(q=q):
                forward_coords(q, o).wait_recv()
                forward(q).wait_recv()
                for l in range(leaves):
                    vs[o, 16 * q + l] = stacked(rv[q, :, l * 256 : (l + 1) * 256])

    first = jnp.full((cols, 128), c, jnp.int32) == 0
    wide = jnp.full((cols, 256), c, jnp.int32) == 0

    def result(t):
        return remote(ns.at[t], nr.at[t], r_send.at[t], r_recv.at[t], d, o)

    def near(t, carry):
        l = c * 4 + t
        points = cs[leaves + l].T
        for k in range(3):
            bx[k, 0:128, :] = jnp.broadcast_to(points[:, k : k + 1], (128, 128))
            bx[k, 128:256, :] = jnp.broadcast_to(points[:, 3 + k : 4 + k], (128, 128))
        total = None
        for j in range(8):
            i = source(near_ref[l, j], (d - 1) * leaves, 24)
            rows = cs[i]
            his, los = [], []
            for h in range(2):
                r2 = None
                for k in range(3):
                    e = bx[k] - rows[3 * h + k : 3 * h + k + 1, :]
                    r2 = e * e if r2 is None else r2 + e * e
                hi, lo = split(lax.rsqrt(r2 + SOFTENING))
                his.append(hi)
                los.append(lo)
            v0, v1 = vs[0, i], vs[1, i]
            v2 = jnp.concatenate([v0[:cols], v1[:cols], v0[cols:], v1[cols:]], 0)
            term = dot3(v2, jnp.concatenate(his, 1), jnp.concatenate(los, 1), NT)
            total = term if total is None else total + term
        total = total * (1.0 / 16.0)
        a, b = total[:cols], total[cols:]
        nk[t] = jnp.where(wide, a, b)
        ns[t] = jnp.where(wide, b, a)
        result(t).start()
        return carry

    for copy in get_lists:
        copy.wait()
    pass_on()
    total = contrib
    for k in range(1, 8):
        remote(sc, zb.at[k], z_send.at[k], z_recv.at[k], d, o).wait_recv()
    for k in range(1, 8):
        total = total + zb[k]
    st[...] = total
    heard(8, 7)
    for k in range(1, 16):
        send(st, tb.at[g], t_send.at[k], t_recv.at[k], lax.rem(g + k, 16) * 8 + z, c)
    tb[g] = total

    def paired(load, i, j):
        rows = []
        for s in range(2):
            a, b = load(s, i), load(s, j)
            rows += [jnp.where(low, a, pltpu.roll(b, 64, 1)), jnp.where(low, pltpu.roll(a, 64, 1), b)]
        return jnp.concatenate(rows, 0)

    def coupled(load, index, blocks):
        slots = blocks.shape[0]
        picked = jnp.concatenate([paired(load, index(j), index(j + 1)) for j in range(0, slots, 2)], 1)
        return dot3(stacked(picked), *split(blocks.reshape(slots * 64, 128)), NN)

    for q, _, _, there in sides:

        @pl.when(there)
        def _(q=q):
            for h in range(2):
                land = pl.ds(16 * q, leaves)
                remote(sm.at[h], em.at[h, land], m_send.at[0, h], m_recv.at[2 * q, h], d, o).wait_recv()
                remote(sn.at[h], en.at[h, 2 * q], n_send.at[0, h], n_recv.at[2 * q, h], d, o).wait_recv()

    remote(sm.at[o], em.at[o, own], m_send.at[2, o], m_recv.at[1, o], d, o).wait_recv()
    remote(sn.at[o], en.at[o, 1], n_send.at[2, o], n_recv.at[1, o], d, o).wait_recv()
    for copy in (get_lcp, get_ncp):
        copy.wait()

    def keep(i, both):
        a, b = both[:cols], both[cols:]
        ox[i] = jnp.where(first, a, b)
        sx[i] = jnp.where(first, b, a)

    for l in range(leaves):
        keep(l, coupled(lambda s, i: em[s, i], lambda j: source(leaf_ref[l, j], (d - 1) * leaves, 24), lcp[l]))
    keep(leaves, coupled(lambda s, i: en[s, i], lambda j: source(node_ref[0, j], d - 1, 3), ncp[0]))
    send(sx, rx, x_send.at[0], x_recv.at[0], d, o)
    remote(tcp.at[o], tcp.at[o], x_send.at[1], x_recv.at[1], d, o).wait_recv()
    for j in range(4):
        for h in range(2):
            rows = pl.ds(j * 128 + h * 64, 64)
            tth[rows], ttl[rows] = split(tcp[h, j])

    take_points()
    lax.fori_loop(0, 4, near, 0)

    remote(sx, rx, x_send.at[0], x_recv.at[0], d, o).wait_recv()
    for k in range(1, 16):
        remote(st, tb.at[g], t_send.at[k], t_recv.at[k], d, o).wait_recv()
    picked = jnp.concatenate([tb[source(top_ref[j, g], 0, 16)] for j in range(4)], 1)
    top_local = dot3(stacked(picked), tth[...], ttl[...], NN)
    node_local = ox[leaves] + rx[leaves] + dot3(stacked(top_local), nth[...], ntl[...], NT)
    node2 = stacked(node_local)
    for l in range(leaves):
        leaf_local = ox[l] + rx[l] + dot3(node2, lth[l], ltl[l], NT)
        far = dot3(stacked(leaf_local), bh[l], bl[l], NT)
        out[:, l * 256 : (l + 1) * 256] = far
    for t in range(4):
        result(t).wait_recv()
    for l in range(leaves):
        t, span = l % 4, slice(l * 256, (l + 1) * 256)
        close = jnp.where(wide, nk[t], nr[t]) if l < 4 else jnp.where(wide, nr[t], nk[t])
        out[:, span] = out[:, span] + close
    for copy in sends:
        copy.wait_send()
    for q, leaf, there, _ in sides:

        @pl.when(there)
        def _(q=q, leaf=leaf):
            points = [coords_to(q, leaf), columns_to(q, leaf, 0), columns_to(q, leaf, 1)]
            for copy in (*points, *moments_to(q, leaf)):
                copy.wait_send()

    for q, _, _, there in sides:

        @pl.when(there)
        def _(q=q):
            forward(q).wait_send()
            forward_coords(q, c).wait_send()

    for t in range(4):
        result(t).wait_send()


def body(
    coords, values, leaf_basis, leaf_transfer, node_transfer, leaf_coupling, node_coupling, top_coupling,
    near_list, leaf_list, node_list, top_list,
):
    cols = values.shape[0]
    any_ref = pl.BlockSpec(memory_space=pl.ANY)
    vmem = pl.BlockSpec(memory_space=pltpu.VMEM)
    dma = pltpu.SemaphoreType.DMA
    return pl.pallas_call(
        kernel,
        out_shape=pltpu.VMEM(values.shape, F32),
        in_specs=[any_ref] * 12,
        out_specs=vmem,
        scratch_shapes=[
            pltpu.SMEM((8, 8), jnp.int32),
            pltpu.SMEM((8, 8), jnp.int32),
            pltpu.SMEM((1, 2), jnp.int32),
            pltpu.SMEM((4, 16), jnp.int32),
            pltpu.VMEM((3, 2048), F32),
            pltpu.VMEM((cols, 2048), F32),
            pltpu.VMEM((2, cols, 2048), F32),
            pltpu.VMEM((25, 8, 128), F32),
            pltpu.VMEM((3, cols, 2048), F32),
            pltpu.VMEM((2, 25, 2 * cols, 256), BF16),
            pltpu.VMEM((4, cols, 256), F32),
            pltpu.VMEM((4, cols, 256), F32),
            pltpu.VMEM((4, cols, 256), F32),
            pltpu.VMEM((3, 256, 128), F32),
            pltpu.VMEM((2, 25, 8, 128), F32),
            pltpu.VMEM((2, 4, 8, 128), F32),
            pltpu.VMEM((8, cols, 128), F32),
            pltpu.VMEM((17, cols, 128), F32),
            pltpu.VMEM((2, 8, 8, 128), F32),
            pltpu.VMEM((2, 8, 128), F32),
            pltpu.VMEM((cols, 128), F32),
            pltpu.VMEM((cols, 128), F32),
            pltpu.VMEM((8, 256, 128), F32),
            pltpu.VMEM((8, 128, 128), F32),
            pltpu.VMEM((1, 128, 128), F32),
            pltpu.VMEM((8, 8, 64, 128), F32),
            pltpu.VMEM((1, 2, 64, 128), F32),
            pltpu.VMEM((2, 4, 64, 128), F32),
            pltpu.VMEM((8, 256, 128), BF16),
            pltpu.VMEM((8, 256, 128), BF16),
            pltpu.VMEM((8, 128, 128), BF16),
            pltpu.VMEM((8, 128, 128), BF16),
            pltpu.VMEM((128, 128), BF16),
            pltpu.VMEM((128, 128), BF16),
            pltpu.VMEM((512, 128), BF16),
            pltpu.VMEM((512, 128), BF16),
            pltpu.VMEM((9, cols, 128), F32),
            pltpu.VMEM((9, cols, 128), F32),
            pltpu.VMEM((9, cols, 128), F32),
            dma((13,)),
            dma((2, 2)), dma((2, 2)), dma((2,)), dma((2,)),
            dma((3, 2)), dma((3, 2)), dma((3, 2)), dma((3, 2)),
            dma((8,)), dma((8,)), dma((16,)), dma((16,)),
            dma((2,)), dma((2,)), dma((3,)), dma((3,)), dma((2,)), dma((2,)), dma((4,)), dma((4,)), pltpu.SemaphoreType.REGULAR((9,)), pltpu.SemaphoreType.REGULAR((4,)),
        ],
        compiler_params=pltpu.CompilerParams(collective_id=0, has_side_effects=True),
    )(
        near_list, leaf_list, node_list, top_list.T, coords, values,
        leaf_basis, leaf_transfer, node_transfer, leaf_coupling, node_coupling, top_coupling,
    )


def solution(mesh):
    in_specs = (
        P(None, "leaf"),
        P("col", "leaf"),
        P("leaf", None, None),
        P("leaf", None, None),
        P("leaf", None, None),
        P("leaf", None, "col", None),
        P("leaf", None, "col", None),
        P(None, None, "col", None),
        P("leaf", None),
        P("leaf", None),
        P("leaf", None),
        P(),
    )
    return jax.shard_map(body, mesh=mesh, in_specs=in_specs, out_specs=P("col", "leaf"), check_vma=False)
```

```python
import functools

import jax
import jax.numpy as jnp
from jax import lax
from jax.experimental import pallas as pl
from jax.experimental.pallas import tpu as pltpu
from jax.sharding import PartitionSpec as P

SOFTENING = 0.01
F32, BF16 = jnp.float32, jnp.bfloat16
MESH = pl.DeviceIdType.MESH
NN = (((1,), (0,)), ((), ()))
NT = (((1,), (1,)), ((), ()))


def mm(a, b, dims):
    return lax.dot_general(a, b, dims, preferred_element_type=F32)


def split(x):
    hi = x.astype(BF16)
    return hi, (x - hi.astype(F32)).astype(BF16)


def stacked(x):
    return jnp.concatenate(split(x), axis=0)


def dot3(x2, yh, yl, dims):
    m = x2.shape[0] // 2
    both = mm(x2, yh, dims)
    return both[:m] + both[m:] + mm(x2[:m], yl, dims)


def kernel(
    near_hbm, leaf_hbm, node_hbm, top_hbm, coords_hbm,
    values_hbm, basis_hbm, ltr_hbm, ntr_hbm, lcp_hbm, ncp_hbm, tcp_hbm,
    out,
    near_ref, leaf_ref, node_ref, top_ref, coords,
    vals, ev, cs, rv, vs, nk, ns, nr, bx, em, en, zb, tb, sm, sn, sc, st,
    basis, ltr, ntr, lcp, ncp, tcp, bh, bl, lth, ltl, nth, ntl, tth, ttl,
    ox, sx, rx,
    local_sem, v_send, v_recv, c_send, c_recv, m_send, m_recv, n_send, n_recv,
    z_send, z_recv, t_send, t_recv, x_send, x_recv, f_send, f_recv, g_send, g_recv, r_send, r_recv, tokens, answers,
):
    leaves, chips = 8, 128
    cols = vals.shape[0]
    d, c = lax.axis_index("leaf"), lax.axis_index("col")
    o = 1 - c
    z, g = lax.rem(d, 8), lax.div(d, 8)
    after, before = lax.rem(d + 1, chips), lax.rem(d + chips - 1, chips)

    def fetch(i, src, dst):
        copy = pltpu.make_async_copy(src, dst, local_sem.at[i])
        copy.start()
        return copy

    get_values = fetch(0, values_hbm, vals)
    quarters = [pl.ds(4 * i, 4) for i in range(2)]
    get_basis = [fetch(1 + i, basis_hbm.at[q], basis.at[q]) for i, q in enumerate(quarters)]
    get_ltr = fetch(3, ltr_hbm, ltr)
    get_ntr = fetch(4, ntr_hbm, ntr)
    get_coords = fetch(5, coords_hbm, coords)
    get_tcp = fetch(6, tcp_hbm.at[g], tcp.at[c])
    get_lists = [
        fetch(7 + i, src, dst)
        for i, (src, dst) in enumerate(
            ((near_hbm, near_ref), (leaf_hbm, leaf_ref), (node_hbm, node_ref), (top_hbm, top_ref))
        )
    ]
    get_lcp = fetch(11, lcp_hbm, lcp)
    get_ncp = fetch(12, ncp_hbm, ncp)

    barrier = pltpu.get_barrier_semaphore()

    def greet(leaf, col):
        pl.semaphore_signal(barrier, inc=1, device_id=(leaf, col), device_id_type=MESH)

    def chip(x, y, z):
        return (lax.rem(x, 4) * 4 + lax.rem(y, 4)) * 8 + lax.rem(z, 8)

    x, y = lax.div(g, 4), lax.rem(g, 4)
    x_up, x_down = chip(x + 1, y, z), chip(x + 3, y, z)
    y_up, y_down = chip(x, y + 1, z), chip(x, y + 3, z)
    z_up, z_down = chip(x, y, z + 1), chip(x, y, z + 7)
    no_after, no_before = lax.div(d, chips - 1), lax.div(chips - 1 - d, chips - 1)
    sides = ((0, after, no_after == 0, no_before == 0), (1, before, no_before == 0, no_after == 0))

    greet(d, o)
    greet(z_up, c)
    greet(z_down, c)
    for _, leaf, there, _ in sides:

        @pl.when(there)
        def _(leaf=leaf):
            greet(leaf, 0)
            greet(leaf, 1)

    def relation(mine, theirs, leaf, farther):
        return mine, theirs, leaf, farther, jnp.logical_not(farther)

    relations = (
        relation(0, 1, x_up, x < 3),
        relation(1, 0, x_down, x == 0),
        relation(2, 3, y_up, y < 3),
        relation(3, 2, y_down, y == 0),
    )
    for _, _, leaf, far, _ in relations:

        @pl.when(far)
        def _(leaf=leaf):
            greet(leaf, c)

    greeters = sum(near.astype(jnp.int32) for *_, near in relations)

    def answer():
        for _, theirs, leaf, _, near in relations:

            @pl.when(near)
            def _(theirs=theirs, leaf=leaf):
                pl.semaphore_signal(answers.at[theirs], inc=1, device_id=(leaf, c), device_id_type=MESH)

    def known():
        for mine, _, _, far, _ in relations:

            @pl.when(far)
            def _(mine=mine):
                pl.semaphore_wait(answers.at[mine], 1)

    def token(i, leaf):
        pl.semaphore_signal(tokens.at[i], inc=1, device_id=(leaf, c), device_id_type=MESH)

    def heard(*which):
        for i in which:
            pl.semaphore_wait(tokens.at[i], 1)

    def remote(src, dst, ssem, rsem, leaf, col):
        return pltpu.make_async_remote_copy(
            src_ref=src, dst_ref=dst, send_sem=ssem, recv_sem=rsem,
            device_id=(leaf, col), device_id_type=MESH,
        )

    sends = []

    def send(*args):
        copy = remote(*args)
        copy.start()
        sends.append(copy)

    own = pl.ds(leaves, leaves)
    zero8 = jnp.zeros((8, 128), F32)

    def columns_to(q, leaf, part):
        rows = pl.ds(part * 8, 8)
        return remote(vals.at[rows], ev.at[q, rows], v_send.at[q, part], v_recv.at[q, part], leaf, c)

    def coords_to(q, leaf):
        mine, land = pl.ds(leaves + 4 * c, 4), pl.ds(16 * q + 4 * c, 4)
        return remote(cs.at[mine], cs.at[land], c_send.at[q], c_recv.at[q], leaf, c)

    def moments_to(q, leaf):
        land = pl.ds(16 * q, leaves)
        return [
            copy
            for h in range(2)
            for copy in (
                remote(sn.at[h], en.at[c, 2 * q], n_send.at[q, h], n_recv.at[2 * q, c], leaf, h),
                remote(sm.at[h], em.at[c, land], m_send.at[q, h], m_recv.at[2 * q, c], leaf, h),
            )
        ]

    get_coords.wait()
    for l in range(leaves):
        for h in range(2):
            start = l * 256 + h * 128
            cs[leaves + l, 3 * h : 3 * h + 3, :] = coords[:, start : start + 128]
        cs[leaves + l, 6:8, :] = zero8[:2]
    get_values.wait()
    pl.semaphore_wait(barrier, 7 - 2 * no_after - 2 * no_before + greeters)
    for q, leaf, there, _ in sides:

        @pl.when(there)
        def _(q=q, leaf=leaf):
            coords_to(q, leaf).start()
            columns_to(q, leaf, 0).start()
            columns_to(q, leaf, 1).start()

    send(vals, rv.at[2], f_send.at[2], f_recv.at[2], d, o)
    token(0, z_up)
    token(3, z_down)
    answer()

    for l in range(leaves):
        vs[c, leaves + l] = stacked(vals[:, l * 256 : (l + 1) * 256])
    moments = []
    for l in range(leaves):
        if l % 4 == 0:
            get_basis[l // 4].wait()
        hi, lo = split(basis[l])
        bh[l], bl[l] = hi, lo
        moments.append(dot3(vs[c, leaves + l], hi, lo, NN))
    get_ltr.wait()
    lth[...], ltl[...] = split(ltr[...])
    down = (leaves * 128, 128)
    node = dot3(stacked(jnp.concatenate(moments, 1)), lth[...].reshape(down), ltl[...].reshape(down), NN)
    get_ntr.wait()
    nth[...], ntl[...] = split(ntr[0])
    contrib = dot3(stacked(node), nth[...], ntl[...], NN)
    sc[...] = contrib
    low = lax.broadcasted_iota(jnp.int32, (8, 128), 1) < 64

    def half(x, h):
        a, b = x[:8], x[8:]
        return jnp.where(low, a, pltpu.roll(b, 64, 1)) if h == 0 else jnp.where(low, pltpu.roll(a, 64, 1), b)

    for h in range(2):
        sn[h] = half(node, h)
        for l in range(leaves):
            sm[h, l] = half(moments[l], h)
    for q, leaf, there, _ in sides:

        @pl.when(there)
        def _(q=q, leaf=leaf):
            for copy in moments_to(q, leaf):
                copy.start()

    heard(0)
    token(1, z_up)
    heard(3)
    token(4, z_down)
    heard(1)
    token(2, z_up)
    heard(2)
    for k in (4, 5, 6, 7, 1):
        send(sc, zb.at[k], z_send.at[k], z_recv.at[k], g * 8 + lax.rem(z + k, 8), c)
    heard(4)
    for k in (2, 3):
        send(sc, zb.at[k], z_send.at[k], z_recv.at[k], g * 8 + lax.rem(z + k, 8), c)

    send(sm.at[o], em.at[c, own], m_send.at[2, o], m_recv.at[1, c], d, o)
    send(sn.at[o], en.at[c, 1], n_send.at[2, o], n_recv.at[1, c], d, o)
    get_tcp.wait()
    send(tcp.at[c], tcp.at[c], x_send.at[1], x_recv.at[1], d, o)
    known()
    token(5, x_down)
    em[c, own] = sm[c]
    en[c, 1] = sn[c]

    heard(5)
    token(6, y_up)
    token(8, y_down)
    heard(6)
    token(7, y_up)
    cs[24] = zero8
    tb[16] = jnp.zeros((cols, 128), F32)
    for s in range(2):
        vs[s, 24] = jnp.zeros((2 * cols, 256), BF16)
        em[s, 24] = zero8
        en[s, 3] = zero8

    def source(v, first, none):
        return jnp.where(v >= 0, jnp.clip(v - first, 0, none - 1), none)

    def forward(q):
        return remote(ev.at[q], rv.at[q], f_send.at[q], f_recv.at[q], d, o)

    def forward_coords(q, core):
        land = cs.at[pl.ds(16 * q + 4 * core, 4)]
        return remote(land, land, g_send.at[q], g_recv.at[q], d, o)

    def pass_on():
        for q, leaf, _, there in sides:

            @pl.when(there)
            def _(q=q, leaf=leaf):
                coords_to(q, leaf).wait_recv()
                forward_coords(q, c).start()
                for part in range(2):
                    columns_to(q, leaf, part).wait_recv()
                forward(q).start()

    def take_points():
        for q, _, _, there in sides:

            @pl.when(there)
            def _(q=q):
                for l in range(leaves):
                    vs[c, 16 * q + l] = stacked(ev[q, :, l * 256 : (l + 1) * 256])

        remote(vals, rv.at[2], f_send.at[2], f_recv.at[2], d, o).wait_recv()
        for l in range(leaves):
            vs[o, leaves + l] = stacked(rv[2, :, l * 256 : (l + 1) * 256])
        for q, _, _, there in sides:

            @pl.when(there)
            def _(q=q):
                forward_coords(q, o).wait_recv()
                forward(q).wait_recv()
                for l in range(leaves):
                    vs[o, 16 * q + l] = stacked(rv[q, :, l * 256 : (l + 1) * 256])

    first = jnp.full((cols, 128), c, jnp.int32) == 0
    wide = jnp.full((cols, 256), c, jnp.int32) == 0

    def result(t):
        return remote(ns.at[t], nr.at[t], r_send.at[t], r_recv.at[t], d, o)

    def near(t, carry):
        l = c * 4 + t
        points = cs[leaves + l].T
        for k in range(3):
            bx[k, 0:128, :] = jnp.broadcast_to(points[:, k : k + 1], (128, 128))
            bx[k, 128:256, :] = jnp.broadcast_to(points[:, 3 + k : 4 + k], (128, 128))
        total = None
        for j in range(8):
            i = source(near_ref[l, j], (d - 1) * leaves, 24)
            rows = cs[i]
            his, los = [], []
            for h in range(2):
                r2 = None
                for k in range(3):
                    e = bx[k] - rows[3 * h + k : 3 * h + k + 1, :]
                    r2 = e * e if r2 is None else r2 + e * e
                hi, lo = split(lax.rsqrt(r2 + SOFTENING))
                his.append(hi)
                los.append(lo)
            v0, v1 = vs[0, i], vs[1, i]
            v2 = jnp.concatenate([v0[:cols], v1[:cols], v0[cols:], v1[cols:]], 0)
            term = dot3(v2, jnp.concatenate(his, 1), jnp.concatenate(los, 1), NT)
            total = term if total is None else total + term
        total = total * (1.0 / 16.0)
        a, b = total[:cols], total[cols:]
        nk[t] = jnp.where(wide, a, b)
        ns[t] = jnp.where(wide, b, a)
        result(t).start()
        return carry

    for copy in get_lists:
        copy.wait()
    pass_on()
    total = contrib
    for k in range(1, 8):
        remote(sc, zb.at[k], z_send.at[k], z_recv.at[k], d, o).wait_recv()
    for k in range(1, 8):
        total = total + zb[k]
    st[...] = total
    heard(8, 7)
    for k in range(1, 16):
        send(st, tb.at[g], t_send.at[k], t_recv.at[k], lax.rem(g + k, 16) * 8 + z, c)
    tb[g] = total

    def paired(load, i, j):
        rows = []
        for s in range(2):
            a, b = load(s, i), load(s, j)
            rows += [jnp.where(low, a, pltpu.roll(b, 64, 1)), jnp.where(low, pltpu.roll(a, 64, 1), b)]
        return jnp.concatenate(rows, 0)

    def coupled(load, index, blocks):
        slots = blocks.shape[0]
        picked = jnp.concatenate([paired(load, index(j), index(j + 1)) for j in range(0, slots, 2)], 1)
        return dot3(stacked(picked), *split(blocks.reshape(slots * 64, 128)), NN)

    for q, _, _, there in sides:

        @pl.when(there)
        def _(q=q):
            for h in range(2):
                land = pl.ds(16 * q, leaves)
                remote(sm.at[h], em.at[h, land], m_send.at[0, h], m_recv.at[2 * q, h], d, o).wait_recv()
                remote(sn.at[h], en.at[h, 2 * q], n_send.at[0, h], n_recv.at[2 * q, h], d, o).wait_recv()

    remote(sm.at[o], em.at[o, own], m_send.at[2, o], m_recv.at[1, o], d, o).wait_recv()
    remote(sn.at[o], en.at[o, 1], n_send.at[2, o], n_recv.at[1, o], d, o).wait_recv()
    for copy in (get_lcp, get_ncp):
        copy.wait()

    def keep(i, both):
        a, b = both[:cols], both[cols:]
        ox[i] = jnp.where(first, a, b)
        sx[i] = jnp.where(first, b, a)

    for l in range(leaves):
        keep(l, coupled(lambda s, i: em[s, i], lambda j: source(leaf_ref[l, j], (d - 1) * leaves, 24), lcp[l]))
    keep(leaves, coupled(lambda s, i: en[s, i], lambda j: source(node_ref[0, j], d - 1, 3), ncp[0]))
    send(sx, rx, x_send.at[0], x_recv.at[0], d, o)
    remote(tcp.at[o], tcp.at[o], x_send.at[1], x_recv.at[1], d, o).wait_recv()
    for j in range(4):
        for h in range(2):
            rows = pl.ds(j * 128 + h * 64, 64)
            tth[rows], ttl[rows] = split(tcp[h, j])

    take_points()
    lax.fori_loop(0, 4, near, 0)

    remote(sx, rx, x_send.at[0], x_recv.at[0], d, o).wait_recv()
    for k in range(1, 16):
        remote(st, tb.at[g], t_send.at[k], t_recv.at[k], d, o).wait_recv()
    picked = jnp.concatenate([tb[source(top_ref[j, g], 0, 16)] for j in range(4)], 1)
    top_local = dot3(stacked(picked), tth[...], ttl[...], NN)
    node_local = ox[leaves] + rx[leaves] + dot3(stacked(top_local), nth[...], ntl[...], NT)
    node2 = stacked(node_local)
    for l in range(leaves):
        leaf_local = ox[l] + rx[l] + dot3(node2, lth[l], ltl[l], NT)
        far = dot3(stacked(leaf_local), bh[l], bl[l], NT)
        out[:, l * 256 : (l + 1) * 256] = far
    for t in range(4):
        result(t).wait_recv()
    for l in range(leaves):
        t, span = l % 4, slice(l * 256, (l + 1) * 256)
        close = jnp.where(wide, nk[t], nr[t]) if l < 4 else jnp.where(wide, nr[t], nk[t])
        out[:, span] = out[:, span] + close
    for copy in sends:
        copy.wait_send()
    for q, leaf, there, _ in sides:

        @pl.when(there)
        def _(q=q, leaf=leaf):
            points = [coords_to(q, leaf), columns_to(q, leaf, 0), columns_to(q, leaf, 1)]
            for copy in (*points, *moments_to(q, leaf)):
                copy.wait_send()

    for q, _, _, there in sides:

        @pl.when(there)
        def _(q=q):
            forward(q).wait_send()
            forward_coords(q, c).wait_send()

    for t in range(4):
        result(t).wait_send()


def body(
    coords, values, leaf_basis, leaf_transfer, node_transfer, leaf_coupling, node_coupling, top_coupling,
    near_list, leaf_list, node_list, top_list,
):
    cols = values.shape[0]
    any_ref = pl.BlockSpec(memory_space=pl.ANY)
    vmem = pl.BlockSpec(memory_space=pltpu.VMEM)
    dma = pltpu.SemaphoreType.DMA
    return pl.pallas_call(
        kernel,
        out_shape=pltpu.VMEM(values.shape, F32),
        in_specs=[any_ref] * 12,
        out_specs=vmem,
        scratch_shapes=[
            pltpu.SMEM((8, 8), jnp.int32),
            pltpu.SMEM((8, 8), jnp.int32),
            pltpu.SMEM((1, 2), jnp.int32),
            pltpu.SMEM((4, 16), jnp.int32),
            pltpu.VMEM((3, 2048), F32),
            pltpu.VMEM((cols, 2048), F32),
            pltpu.VMEM((2, cols, 2048), F32),
            pltpu.VMEM((25, 8, 128), F32),
            pltpu.VMEM((3, cols, 2048), F32),
            pltpu.VMEM((2, 25, 2 * cols, 256), BF16),
            pltpu.VMEM((4, cols, 256), F32),
            pltpu.VMEM((4, cols, 256), F32),
            pltpu.VMEM((4, cols, 256), F32),
            pltpu.VMEM((3, 256, 128), F32),
            pltpu.VMEM((2, 25, 8, 128), F32),
            pltpu.VMEM((2, 4, 8, 128), F32),
            pltpu.VMEM((8, cols, 128), F32),
            pltpu.VMEM((17, cols, 128), F32),
            pltpu.VMEM((2, 8, 8, 128), F32),
            pltpu.VMEM((2, 8, 128), F32),
            pltpu.VMEM((cols, 128), F32),
            pltpu.VMEM((cols, 128), F32),
            pltpu.VMEM((8, 256, 128), F32),
            pltpu.VMEM((8, 128, 128), F32),
            pltpu.VMEM((1, 128, 128), F32),
            pltpu.VMEM((8, 8, 64, 128), F32),
            pltpu.VMEM((1, 2, 64, 128), F32),
            pltpu.VMEM((2, 4, 64, 128), F32),
            pltpu.VMEM((8, 256, 128), BF16),
            pltpu.VMEM((8, 256, 128), BF16),
            pltpu.VMEM((8, 128, 128), BF16),
            pltpu.VMEM((8, 128, 128), BF16),
            pltpu.VMEM((128, 128), BF16),
            pltpu.VMEM((128, 128), BF16),
            pltpu.VMEM((512, 128), BF16),
            pltpu.VMEM((512, 128), BF16),
            pltpu.VMEM((9, cols, 128), F32),
            pltpu.VMEM((9, cols, 128), F32),
            pltpu.VMEM((9, cols, 128), F32),
            dma((13,)),
            dma((2, 2)), dma((2, 2)), dma((2,)), dma((2,)),
            dma((3, 2)), dma((3, 2)), dma((3, 2)), dma((3, 2)),
            dma((8,)), dma((8,)), dma((16,)), dma((16,)),
            dma((2,)), dma((2,)), dma((3,)), dma((3,)), dma((2,)), dma((2,)), dma((4,)), dma((4,)), pltpu.SemaphoreType.REGULAR((9,)), pltpu.SemaphoreType.REGULAR((4,)),
        ],
        compiler_params=pltpu.CompilerParams(collective_id=0, has_side_effects=True),
    )(
        near_list, leaf_list, node_list, top_list.T, coords, values,
        leaf_basis, leaf_transfer, node_transfer, leaf_coupling, node_coupling, top_coupling,
    )


def solution(mesh):
    in_specs = (
        P(None, "leaf"),
        P("col", "leaf"),
        P("leaf", None, None),
        P("leaf", None, None),
        P("leaf", None, None),
        P("leaf", None, "col", None),
        P("leaf", None, "col", None),
        P(None, None, "col", None),
        P("leaf", None),
        P("leaf", None),
        P("leaf", None),
        P(),
    )
    return jax.shard_map(body, mesh=mesh, in_specs=in_specs, out_specs=P("col", "leaf"), check_vma=False)
```

```python
import functools

import jax
import jax.numpy as jnp
from jax import lax
from jax.experimental import pallas as pl
from jax.experimental.pallas import tpu as pltpu
from jax.sharding import PartitionSpec as P

SOFTENING = 0.01
F32, BF16 = jnp.float32, jnp.bfloat16
MESH = pl.DeviceIdType.MESH
NN = (((1,), (0,)), ((), ()))
NT = (((1,), (1,)), ((), ()))


def mm(a, b, dims):
    return lax.dot_general(a, b, dims, preferred_element_type=F32)


def split(x):
    hi = x.astype(BF16)
    return hi, (x - hi.astype(F32)).astype(BF16)


def stacked(x):
    return jnp.concatenate(split(x), axis=0)


def dot3(x2, yh, yl, dims):
    m = x2.shape[0] // 2
    both = mm(x2, yh, dims)
    return both[:m] + both[m:] + mm(x2[:m], yl, dims)


def kernel(
    near_hbm, leaf_hbm, node_hbm, top_hbm, coords_hbm,
    values_hbm, basis_hbm, ltr_hbm, ntr_hbm, lcp_hbm, ncp_hbm, tcp_hbm,
    out,
    near_ref, leaf_ref, node_ref, top_ref, coords,
    vals, ev, cs, rv, vs, nk, ns, nr, bx, em, en, zb, tb, sm, sn, sc, st,
    basis, ltr, ntr, lcp, ncp, tcp, bh, bl, lth, ltl, nth, ntl, tth, ttl,
    ox, sx, rx,
    local_sem, v_send, v_recv, c_send, c_recv, m_send, m_recv, n_send, n_recv,
    z_send, z_recv, t_send, t_recv, x_send, x_recv, f_send, f_recv, g_send, g_recv, r_send, r_recv, tokens, answers,
):
    leaves, chips = 8, 128
    cols = vals.shape[0]
    d, c = lax.axis_index("leaf"), lax.axis_index("col")
    o = 1 - c
    z, g = lax.rem(d, 8), lax.div(d, 8)
    after, before = lax.rem(d + 1, chips), lax.rem(d + chips - 1, chips)

    def fetch(i, src, dst):
        copy = pltpu.make_async_copy(src, dst, local_sem.at[i])
        copy.start()
        return copy

    get_values = fetch(0, values_hbm, vals)
    quarters = [pl.ds(4 * i, 4) for i in range(2)]
    get_basis = [fetch(1 + i, basis_hbm.at[q], basis.at[q]) for i, q in enumerate(quarters)]
    get_ltr = fetch(3, ltr_hbm, ltr)
    get_ntr = fetch(4, ntr_hbm, ntr)
    get_coords = fetch(5, coords_hbm, coords)
    get_tcp = fetch(6, tcp_hbm.at[g], tcp.at[c])
    get_lists = [
        fetch(7 + i, src, dst)
        for i, (src, dst) in enumerate(
            ((near_hbm, near_ref), (leaf_hbm, leaf_ref), (node_hbm, node_ref), (top_hbm, top_ref))
        )
    ]
    get_lcp = fetch(11, lcp_hbm, lcp)
    get_ncp = fetch(12, ncp_hbm, ncp)

    barrier = pltpu.get_barrier_semaphore()

    def greet(leaf, col):
        pl.semaphore_signal(barrier, inc=1, device_id=(leaf, col), device_id_type=MESH)

    def chip(x, y, z):
        return (lax.rem(x, 4) * 4 + lax.rem(y, 4)) * 8 + lax.rem(z, 8)

    x, y = lax.div(g, 4), lax.rem(g, 4)
    x_up, x_down = chip(x + 1, y, z), chip(x + 3, y, z)
    y_up, y_down = chip(x, y + 1, z), chip(x, y + 3, z)
    z_up, z_down = chip(x, y, z + 1), chip(x, y, z + 7)
    no_after, no_before = lax.div(d, chips - 1), lax.div(chips - 1 - d, chips - 1)
    sides = ((0, after, no_after == 0, no_before == 0), (1, before, no_before == 0, no_after == 0))

    greet(d, o)
    greet(z_up, c)
    greet(z_down, c)
    for _, leaf, there, _ in sides:

        @pl.when(there)
        def _(leaf=leaf):
            greet(leaf, 0)
            greet(leaf, 1)

    def relation(mine, theirs, leaf, farther):
        return mine, theirs, leaf, farther, jnp.logical_not(farther)

    relations = (
        relation(0, 1, x_up, x < 3),
        relation(1, 0, x_down, x == 0),
        relation(2, 3, y_up, y < 3),
        relation(3, 2, y_down, y == 0),
    )
    for _, _, leaf, far, _ in relations:

        @pl.when(far)
        def _(leaf=leaf):
            greet(leaf, c)

    greeters = sum(near.astype(jnp.int32) for *_, near in relations)

    def answer():
        for _, theirs, leaf, _, near in relations:

            @pl.when(near)
            def _(theirs=theirs, leaf=leaf):
                pl.semaphore_signal(answers.at[theirs], inc=1, device_id=(leaf, c), device_id_type=MESH)

    def known():
        for mine, _, _, far, _ in relations:

            @pl.when(far)
            def _(mine=mine):
                pl.semaphore_wait(answers.at[mine], 1)

    def token(i, leaf):
        pl.semaphore_signal(tokens.at[i], inc=1, device_id=(leaf, c), device_id_type=MESH)

    def heard(*which):
        for i in which:
            pl.semaphore_wait(tokens.at[i], 1)

    def remote(src, dst, ssem, rsem, leaf, col):
        return pltpu.make_async_remote_copy(
            src_ref=src, dst_ref=dst, send_sem=ssem, recv_sem=rsem,
            device_id=(leaf, col), device_id_type=MESH,
        )

    sends = []

    def send(*args):
        copy = remote(*args)
        copy.start()
        sends.append(copy)

    own = pl.ds(leaves, leaves)
    zero8 = jnp.zeros((8, 128), F32)

    def columns_to(q, leaf, part):
        rows = pl.ds(part * 8, 8)
        return remote(vals.at[rows], ev.at[q, rows], v_send.at[q, part], v_recv.at[q, part], leaf, c)

    def coords_to(q, leaf):
        mine, land = pl.ds(leaves + 4 * c, 4), pl.ds(16 * q + 4 * c, 4)
        return remote(cs.at[mine], cs.at[land], c_send.at[q], c_recv.at[q], leaf, c)

    def moments_to(q, leaf):
        land = pl.ds(16 * q, leaves)
        return [
            copy
            for h in range(2)
            for copy in (
                remote(sn.at[h], en.at[c, 2 * q], n_send.at[q, h], n_recv.at[2 * q, c], leaf, h),
                remote(sm.at[h], em.at[c, land], m_send.at[q, h], m_recv.at[2 * q, c], leaf, h),
            )
        ]

    pl.semaphore_wait(barrier, 7 - 2 * no_after - 2 * no_before + greeters)
    token(0, z_up)
    token(3, z_down)
    answer()
    get_values.wait()
    for q, leaf, there, _ in sides:

        @pl.when(there)
        def _(q=q, leaf=leaf):
            columns_to(q, leaf, 0).start()
            columns_to(q, leaf, 1).start()

    get_coords.wait()
    for l in range(leaves):
        for h in range(2):
            start = l * 256 + h * 128
            cs[leaves + l, 3 * h : 3 * h + 3, :] = coords[:, start : start + 128]
        cs[leaves + l, 6:8, :] = zero8[:2]
    for q, leaf, there, _ in sides:

        @pl.when(there)
        def _(q=q, leaf=leaf):
            coords_to(q, leaf).start()

    send(vals, rv.at[2], f_send.at[2], f_recv.at[2], d, o)

    for l in range(leaves):
        vs[c, leaves + l] = stacked(vals[:, l * 256 : (l + 1) * 256])
    moments = []
    for l in range(leaves):
        if l % 4 == 0:
            get_basis[l // 4].wait()
        hi, lo = split(basis[l])
        bh[l], bl[l] = hi, lo
        moments.append(dot3(vs[c, leaves + l], hi, lo, NN))
    get_ltr.wait()
    lth[...], ltl[...] = split(ltr[...])
    down = (leaves * 128, 128)
    node = dot3(stacked(jnp.concatenate(moments, 1)), lth[...].reshape(down), ltl[...].reshape(down), NN)
    get_ntr.wait()
    nth[...], ntl[...] = split(ntr[0])
    contrib = dot3(stacked(node), nth[...], ntl[...], NN)
    sc[...] = contrib
    low = lax.broadcasted_iota(jnp.int32, (8, 128), 1) < 64

    def half(x, h):
        a, b = x[:8], x[8:]
        return jnp.where(low, a, pltpu.roll(b, 64, 1)) if h == 0 else jnp.where(low, pltpu.roll(a, 64, 1), b)

    for h in range(2):
        sn[h] = half(node, h)
        for l in range(leaves):
            sm[h, l] = half(moments[l], h)
    for q, leaf, there, _ in sides:

        @pl.when(there)
        def _(q=q, leaf=leaf):
            for copy in moments_to(q, leaf):
                copy.start()

    heard(0)
    token(1, z_up)
    heard(3)
    token(4, z_down)
    heard(1)
    token(2, z_up)
    heard(2)
    for k in (4, 5, 6, 7, 1):
        send(sc, zb.at[k], z_send.at[k], z_recv.at[k], g * 8 + lax.rem(z + k, 8), c)
    heard(4)
    for k in (2, 3):
        send(sc, zb.at[k], z_send.at[k], z_recv.at[k], g * 8 + lax.rem(z + k, 8), c)

    send(sm.at[o], em.at[c, own], m_send.at[2, o], m_recv.at[1, c], d, o)
    send(sn.at[o], en.at[c, 1], n_send.at[2, o], n_recv.at[1, c], d, o)
    get_tcp.wait()
    send(tcp.at[c], tcp.at[c], x_send.at[1], x_recv.at[1], d, o)
    known()
    token(5, x_down)
    em[c, own] = sm[c]
    en[c, 1] = sn[c]

    heard(5)
    token(6, y_up)
    token(8, y_down)
    heard(6)
    token(7, y_up)
    cs[24] = zero8
    tb[16] = jnp.zeros((cols, 128), F32)
    for s in range(2):
        vs[s, 24] = jnp.zeros((2 * cols, 256), BF16)
        em[s, 24] = zero8
        en[s, 3] = zero8

    def source(v, first, none):
        return jnp.where(v >= 0, jnp.clip(v - first, 0, none - 1), none)

    def forward(q):
        return remote(ev.at[q], rv.at[q], f_send.at[q], f_recv.at[q], d, o)

    def forward_coords(q, core):
        land = cs.at[pl.ds(16 * q + 4 * core, 4)]
        return remote(land, land, g_send.at[q], g_recv.at[q], d, o)

    def pass_on():
        for q, leaf, _, there in sides:

            @pl.when(there)
            def _(q=q, leaf=leaf):
                coords_to(q, leaf).wait_recv()
                forward_coords(q, c).start()
                for part in range(2):
                    columns_to(q, leaf, part).wait_recv()
                forward(q).start()

    def take_points():
        for q, _, _, there in sides:

            @pl.when(there)
            def _(q=q):
                for l in range(leaves):
                    vs[c, 16 * q + l] = stacked(ev[q, :, l * 256 : (l + 1) * 256])

        remote(vals, rv.at[2], f_send.at[2], f_recv.at[2], d, o).wait_recv()
        for l in range(leaves):
            vs[o, leaves + l] = stacked(rv[2, :, l * 256 : (l + 1) * 256])
        for q, _, _, there in sides:

            @pl.when(there)
            def _(q=q):
                forward_coords(q, o).wait_recv()
                forward(q).wait_recv()
                for l in range(leaves):
                    vs[o, 16 * q + l] = stacked(rv[q, :, l * 256 : (l + 1) * 256])

    first = jnp.full((cols, 128), c, jnp.int32) == 0
    wide = jnp.full((cols, 256), c, jnp.int32) == 0

    def result(t):
        return remote(ns.at[t], nr.at[t], r_send.at[t], r_recv.at[t], d, o)

    def near(t, carry):
        l = c * 4 + t
        points = cs[leaves + l].T
        for k in range(3):
            bx[k, 0:128, :] = jnp.broadcast_to(points[:, k : k + 1], (128, 128))
            bx[k, 128:256, :] = jnp.broadcast_to(points[:, 3 + k : 4 + k], (128, 128))
        total = None
        for j in range(8):
            i = source(near_ref[l, j], (d - 1) * leaves, 24)
            rows = cs[i]
            his, los = [], []
            for h in range(2):
                r2 = None
                for k in range(3):
                    e = bx[k] - rows[3 * h + k : 3 * h + k + 1, :]
                    r2 = e * e if r2 is None else r2 + e * e
                hi, lo = split(lax.rsqrt(r2 + SOFTENING))
                his.append(hi)
                los.append(lo)
            v0, v1 = vs[0, i], vs[1, i]
            v2 = jnp.concatenate([v0[:cols], v1[:cols], v0[cols:], v1[cols:]], 0)
            term = dot3(v2, jnp.concatenate(his, 1), jnp.concatenate(los, 1), NT)
            total = term if total is None else total + term
        total = total * (1.0 / 16.0)
        a, b = total[:cols], total[cols:]
        nk[t] = jnp.where(wide, a, b)
        ns[t] = jnp.where(wide, b, a)
        result(t).start()
        return carry

    for copy in get_lists:
        copy.wait()
    pass_on()
    total = contrib
    for k in range(1, 8):
        remote(sc, zb.at[k], z_send.at[k], z_recv.at[k], d, o).wait_recv()
    for k in range(1, 8):
        total = total + zb[k]
    st[...] = total
    heard(8, 7)
    far_first = sorted(range(1, 16), key=lambda k: -(min(k // 4, 4 - k // 4) + min(k % 4, 4 - k % 4)))
    for k in far_first:
        send(st, tb.at[g], t_send.at[k], t_recv.at[k], chip(x + k // 4, y + k % 4, z), c)
    tb[g] = total

    def paired(load, i, j):
        rows = []
        for s in range(2):
            a, b = load(s, i), load(s, j)
            rows += [jnp.where(low, a, pltpu.roll(b, 64, 1)), jnp.where(low, pltpu.roll(a, 64, 1), b)]
        return jnp.concatenate(rows, 0)

    def coupled(load, index, blocks):
        slots = blocks.shape[0]
        picked = jnp.concatenate([paired(load, index(j), index(j + 1)) for j in range(0, slots, 2)], 1)
        return dot3(stacked(picked), *split(blocks.reshape(slots * 64, 128)), NN)

    for q, _, _, there in sides:

        @pl.when(there)
        def _(q=q):
            for h in range(2):
                land = pl.ds(16 * q, leaves)
                remote(sm.at[h], em.at[h, land], m_send.at[0, h], m_recv.at[2 * q, h], d, o).wait_recv()
                remote(sn.at[h], en.at[h, 2 * q], n_send.at[0, h], n_recv.at[2 * q, h], d, o).wait_recv()

    remote(sm.at[o], em.at[o, own], m_send.at[2, o], m_recv.at[1, o], d, o).wait_recv()
    remote(sn.at[o], en.at[o, 1], n_send.at[2, o], n_recv.at[1, o], d, o).wait_recv()
    for copy in (get_lcp, get_ncp):
        copy.wait()

    def keep(i, both):
        a, b = both[:cols], both[cols:]
        ox[i] = jnp.where(first, a, b)
        sx[i] = jnp.where(first, b, a)

    for l in range(leaves):
        keep(l, coupled(lambda s, i: em[s, i], lambda j: source(leaf_ref[l, j], (d - 1) * leaves, 24), lcp[l]))
    keep(leaves, coupled(lambda s, i: en[s, i], lambda j: source(node_ref[0, j], d - 1, 3), ncp[0]))
    send(sx, rx, x_send.at[0], x_recv.at[0], d, o)
    remote(tcp.at[o], tcp.at[o], x_send.at[1], x_recv.at[1], d, o).wait_recv()
    for j in range(4):
        for h in range(2):
            rows = pl.ds(j * 128 + h * 64, 64)
            tth[rows], ttl[rows] = split(tcp[h, j])

    take_points()
    lax.fori_loop(0, 4, near, 0)

    remote(sx, rx, x_send.at[0], x_recv.at[0], d, o).wait_recv()
    for k in range(1, 16):
        remote(st, tb.at[g], t_send.at[k], t_recv.at[k], d, o).wait_recv()
    picked = jnp.concatenate([tb[source(top_ref[j, g], 0, 16)] for j in range(4)], 1)
    top_local = dot3(stacked(picked), tth[...], ttl[...], NN)
    node_local = ox[leaves] + rx[leaves] + dot3(stacked(top_local), nth[...], ntl[...], NT)
    node2 = stacked(node_local)
    for l in range(leaves):
        leaf_local = ox[l] + rx[l] + dot3(node2, lth[l], ltl[l], NT)
        far = dot3(stacked(leaf_local), bh[l], bl[l], NT)
        out[:, l * 256 : (l + 1) * 256] = far
    for t in range(4):
        result(t).wait_recv()
    for l in range(leaves):
        t, span = l % 4, slice(l * 256, (l + 1) * 256)
        close = jnp.where(wide, nk[t], nr[t]) if l < 4 else jnp.where(wide, nr[t], nk[t])
        out[:, span] = out[:, span] + close
    for copy in sends:
        copy.wait_send()
    for q, leaf, there, _ in sides:

        @pl.when(there)
        def _(q=q, leaf=leaf):
            points = [coords_to(q, leaf), columns_to(q, leaf, 0), columns_to(q, leaf, 1)]
            for copy in (*points, *moments_to(q, leaf)):
                copy.wait_send()

    for q, _, _, there in sides:

        @pl.when(there)
        def _(q=q):
            forward(q).wait_send()
            forward_coords(q, c).wait_send()

    for t in range(4):
        result(t).wait_send()


def body(
    coords, values, leaf_basis, leaf_transfer, node_transfer, leaf_coupling, node_coupling, top_coupling,
    near_list, leaf_list, node_list, top_list,
):
    cols = values.shape[0]
    any_ref = pl.BlockSpec(memory_space=pl.ANY)
    vmem = pl.BlockSpec(memory_space=pltpu.VMEM)
    dma = pltpu.SemaphoreType.DMA
    return pl.pallas_call(
        kernel,
        out_shape=pltpu.VMEM(values.shape, F32),
        in_specs=[any_ref] * 12,
        out_specs=vmem,
        scratch_shapes=[
            pltpu.SMEM((8, 8), jnp.int32),
            pltpu.SMEM((8, 8), jnp.int32),
            pltpu.SMEM((1, 2), jnp.int32),
            pltpu.SMEM((4, 16), jnp.int32),
            pltpu.VMEM((3, 2048), F32),
            pltpu.VMEM((cols, 2048), F32),
            pltpu.VMEM((2, cols, 2048), F32),
            pltpu.VMEM((25, 8, 128), F32),
            pltpu.VMEM((3, cols, 2048), F32),
            pltpu.VMEM((2, 25, 2 * cols, 256), BF16),
            pltpu.VMEM((4, cols, 256), F32),
            pltpu.VMEM((4, cols, 256), F32),
            pltpu.VMEM((4, cols, 256), F32),
            pltpu.VMEM((3, 256, 128), F32),
            pltpu.VMEM((2, 25, 8, 128), F32),
            pltpu.VMEM((2, 4, 8, 128), F32),
            pltpu.VMEM((8, cols, 128), F32),
            pltpu.VMEM((17, cols, 128), F32),
            pltpu.VMEM((2, 8, 8, 128), F32),
            pltpu.VMEM((2, 8, 128), F32),
            pltpu.VMEM((cols, 128), F32),
            pltpu.VMEM((cols, 128), F32),
            pltpu.VMEM((8, 256, 128), F32),
            pltpu.VMEM((8, 128, 128), F32),
            pltpu.VMEM((1, 128, 128), F32),
            pltpu.VMEM((8, 8, 64, 128), F32),
            pltpu.VMEM((1, 2, 64, 128), F32),
            pltpu.VMEM((2, 4, 64, 128), F32),
            pltpu.VMEM((8, 256, 128), BF16),
            pltpu.VMEM((8, 256, 128), BF16),
            pltpu.VMEM((8, 128, 128), BF16),
            pltpu.VMEM((8, 128, 128), BF16),
            pltpu.VMEM((128, 128), BF16),
            pltpu.VMEM((128, 128), BF16),
            pltpu.VMEM((512, 128), BF16),
            pltpu.VMEM((512, 128), BF16),
            pltpu.VMEM((9, cols, 128), F32),
            pltpu.VMEM((9, cols, 128), F32),
            pltpu.VMEM((9, cols, 128), F32),
            dma((13,)),
            dma((2, 2)), dma((2, 2)), dma((2,)), dma((2,)),
            dma((3, 2)), dma((3, 2)), dma((3, 2)), dma((3, 2)),
            dma((8,)), dma((8,)), dma((16,)), dma((16,)),
            dma((2,)), dma((2,)), dma((3,)), dma((3,)), dma((2,)), dma((2,)), dma((4,)), dma((4,)), pltpu.SemaphoreType.REGULAR((9,)), pltpu.SemaphoreType.REGULAR((4,)),
        ],
        compiler_params=pltpu.CompilerParams(collective_id=0, has_side_effects=True),
    )(
        near_list, leaf_list, node_list, top_list.T, coords, values,
        leaf_basis, leaf_transfer, node_transfer, leaf_coupling, node_coupling, top_coupling,
    )


def solution(mesh):
    in_specs = (
        P(None, "leaf"),
        P("col", "leaf"),
        P("leaf", None, None),
        P("leaf", None, None),
        P("leaf", None, None),
        P("leaf", None, "col", None),
        P("leaf", None, "col", None),
        P(None, None, "col", None),
        P("leaf", None),
        P("leaf", None),
        P("leaf", None),
        P(),
    )
    return jax.shard_map(body, mesh=mesh, in_specs=in_specs, out_specs=P("col", "leaf"), check_vma=False)
```

```python
import functools

import jax
import jax.numpy as jnp
from jax import lax
from jax.experimental import pallas as pl
from jax.experimental.pallas import tpu as pltpu
from jax.sharding import PartitionSpec as P

SOFTENING = 0.01
F32, BF16 = jnp.float32, jnp.bfloat16
MESH = pl.DeviceIdType.MESH
NN = (((1,), (0,)), ((), ()))
NT = (((1,), (1,)), ((), ()))


def mm(a, b, dims):
    return lax.dot_general(a, b, dims, preferred_element_type=F32)


def split(x):
    hi = x.astype(BF16)
    return hi, (x - hi.astype(F32)).astype(BF16)


def stacked(x):
    return jnp.concatenate(split(x), axis=0)


def dot3(x2, yh, yl, dims):
    m = x2.shape[0] // 2
    both = mm(x2, yh, dims)
    return both[:m] + both[m:] + mm(x2[:m], yl, dims)


def kernel(
    near_hbm, leaf_hbm, node_hbm, top_hbm, coords_hbm,
    values_hbm, basis_hbm, ltr_hbm, ntr_hbm, lcp_hbm, ncp_hbm, tcp_hbm,
    out,
    near_ref, leaf_ref, node_ref, top_ref, coords,
    vals, ev, cs, rv, vs, nk, ns, nr, bx, em, en, zb, tb, sm, sn, sc, st,
    basis, ltr, ntr, lcp, ncp, tcp, bh, bl, lth, ltl, nth, ntl, tth, ttl,
    ox, sx, rx,
    local_sem, v_send, v_recv, c_send, c_recv, m_send, m_recv, n_send, n_recv,
    z_send, z_recv, t_send, t_recv, x_send, x_recv, f_send, f_recv, g_send, g_recv, r_send, r_recv, tokens, answers,
):
    leaves, chips = 8, 128
    cols = vals.shape[0]
    d, c = lax.axis_index("leaf"), lax.axis_index("col")
    o = 1 - c
    z, g = lax.rem(d, 8), lax.div(d, 8)
    after, before = lax.rem(d + 1, chips), lax.rem(d + chips - 1, chips)

    def fetch(i, src, dst):
        copy = pltpu.make_async_copy(src, dst, local_sem.at[i])
        copy.start()
        return copy

    get_values = fetch(0, values_hbm, vals)
    quarters = [pl.ds(4 * i, 4) for i in range(2)]
    get_basis = [fetch(1 + i, basis_hbm.at[q], basis.at[q]) for i, q in enumerate(quarters)]
    get_ltr = fetch(3, ltr_hbm, ltr)
    get_ntr = fetch(4, ntr_hbm, ntr)
    get_coords = fetch(5, coords_hbm, coords)
    get_tcp = fetch(6, tcp_hbm.at[g], tcp.at[c])
    get_lists = [
        fetch(7 + i, src, dst)
        for i, (src, dst) in enumerate(
            ((near_hbm, near_ref), (leaf_hbm, leaf_ref), (node_hbm, node_ref), (top_hbm, top_ref))
        )
    ]
    get_lcp = fetch(11, lcp_hbm, lcp)
    get_ncp = fetch(12, ncp_hbm, ncp)

    barrier = pltpu.get_barrier_semaphore()

    def greet(leaf, col):
        pl.semaphore_signal(barrier, inc=1, device_id=(leaf, col), device_id_type=MESH)

    def chip(x, y, z):
        return (lax.rem(x, 4) * 4 + lax.rem(y, 4)) * 8 + lax.rem(z, 8)

    x, y = lax.div(g, 4), lax.rem(g, 4)
    x_up, x_down = chip(x + 1, y, z), chip(x + 3, y, z)
    y_up, y_down = chip(x, y + 1, z), chip(x, y + 3, z)
    z_up, z_down = chip(x, y, z + 1), chip(x, y, z + 7)
    no_after, no_before = lax.div(d, chips - 1), lax.div(chips - 1 - d, chips - 1)
    sides = ((0, after, no_after == 0, no_before == 0), (1, before, no_before == 0, no_after == 0))

    greet(d, o)
    greet(z_up, c)
    greet(z_down, c)
    for _, leaf, there, _ in sides:

        @pl.when(there)
        def _(leaf=leaf):
            greet(leaf, 0)
            greet(leaf, 1)

    def relation(mine, theirs, leaf, farther):
        return mine, theirs, leaf, farther, jnp.logical_not(farther)

    relations = (
        relation(0, 1, x_up, x < 3),
        relation(1, 0, x_down, x == 0),
        relation(2, 3, y_up, y < 3),
        relation(3, 2, y_down, y == 0),
    )
    for _, _, leaf, far, _ in relations:

        @pl.when(far)
        def _(leaf=leaf):
            greet(leaf, c)

    greeters = sum(near.astype(jnp.int32) for *_, near in relations)

    def answer():
        for _, theirs, leaf, _, near in relations:

            @pl.when(near)
            def _(theirs=theirs, leaf=leaf):
                pl.semaphore_signal(answers.at[theirs], inc=1, device_id=(leaf, c), device_id_type=MESH)

    def known():
        for mine, _, _, far, _ in relations:

            @pl.when(far)
            def _(mine=mine):
                pl.semaphore_wait(answers.at[mine], 1)

    def token(i, leaf):
        pl.semaphore_signal(tokens.at[i], inc=1, device_id=(leaf, c), device_id_type=MESH)

    def heard(*which):
        for i in which:
            pl.semaphore_wait(tokens.at[i], 1)

    def remote(src, dst, ssem, rsem, leaf, col):
        return pltpu.make_async_remote_copy(
            src_ref=src, dst_ref=dst, send_sem=ssem, recv_sem=rsem,
            device_id=(leaf, col), device_id_type=MESH,
        )

    sends = []

    def send(*args):
        copy = remote(*args)
        copy.start()
        sends.append(copy)

    own = pl.ds(leaves, leaves)
    zero8 = jnp.zeros((8, 128), F32)

    def columns_to(q, leaf, part):
        rows = pl.ds(part * 8, 8)
        return remote(vals.at[rows], ev.at[q, rows], v_send.at[q, part], v_recv.at[q, part], leaf, c)

    def coords_to(q, leaf):
        mine, land = pl.ds(leaves + 4 * c, 4), pl.ds(16 * q + 4 * c, 4)
        return remote(cs.at[mine], cs.at[land], c_send.at[q], c_recv.at[q], leaf, c)

    def moments_to(q, leaf):
        land = pl.ds(16 * q, leaves)
        return [
            copy
            for h in range(2)
            for copy in (
                remote(sn.at[h], en.at[c, 2 * q], n_send.at[q, h], n_recv.at[2 * q, c], leaf, h),
                remote(sm.at[h], em.at[c, land], m_send.at[q, h], m_recv.at[2 * q, c], leaf, h),
            )
        ]

    pl.semaphore_wait(barrier, 7 - 2 * no_after - 2 * no_before + greeters)
    token(0, z_up)
    token(3, z_down)
    answer()
    get_values.wait()
    for q, leaf, there, _ in sides:

        @pl.when(there)
        def _(q=q, leaf=leaf):
            columns_to(q, leaf, 0).start()
            columns_to(q, leaf, 1).start()

    get_coords.wait()
    for l in range(leaves):
        for h in range(2):
            start = l * 256 + h * 128
            cs[leaves + l, 3 * h : 3 * h + 3, :] = coords[:, start : start + 128]
        cs[leaves + l, 6:8, :] = zero8[:2]
    for q, leaf, there, _ in sides:

        @pl.when(there)
        def _(q=q, leaf=leaf):
            coords_to(q, leaf).start()

    send(vals, rv.at[2], f_send.at[2, 0], f_recv.at[2, 0], d, o)

    for l in range(leaves):
        vs[c, leaves + l] = stacked(vals[:, l * 256 : (l + 1) * 256])
    moments = []
    for l in range(leaves):
        if l % 4 == 0:
            get_basis[l // 4].wait()
        hi, lo = split(basis[l])
        bh[l], bl[l] = hi, lo
        moments.append(dot3(vs[c, leaves + l], hi, lo, NN))
    get_ltr.wait()
    lth[...], ltl[...] = split(ltr[...])
    down = (leaves * 128, 128)
    node = dot3(stacked(jnp.concatenate(moments, 1)), lth[...].reshape(down), ltl[...].reshape(down), NN)
    get_ntr.wait()
    nth[...], ntl[...] = split(ntr[0])
    contrib = dot3(stacked(node), nth[...], ntl[...], NN)
    sc[...] = contrib
    low = lax.broadcasted_iota(jnp.int32, (8, 128), 1) < 64

    def half(x, h):
        a, b = x[:8], x[8:]
        return jnp.where(low, a, pltpu.roll(b, 64, 1)) if h == 0 else jnp.where(low, pltpu.roll(a, 64, 1), b)

    for h in range(2):
        sn[h] = half(node, h)
        for l in range(leaves):
            sm[h, l] = half(moments[l], h)
    for q, leaf, there, _ in sides:

        @pl.when(there)
        def _(q=q, leaf=leaf):
            for copy in moments_to(q, leaf):
                copy.start()

    heard(0)
    token(1, z_up)
    heard(3)
    token(4, z_down)
    heard(1)
    token(2, z_up)
    heard(2)
    for k in (4, 5, 6, 7, 1):
        send(sc, zb.at[k], z_send.at[k], z_recv.at[k], g * 8 + lax.rem(z + k, 8), c)
    heard(4)
    for k in (2, 3):
        send(sc, zb.at[k], z_send.at[k], z_recv.at[k], g * 8 + lax.rem(z + k, 8), c)

    send(sm.at[o], em.at[c, own], m_send.at[2, o], m_recv.at[1, c], d, o)
    send(sn.at[o], en.at[c, 1], n_send.at[2, o], n_recv.at[1, c], d, o)
    get_tcp.wait()
    send(tcp.at[c], tcp.at[c], x_send.at[1], x_recv.at[1], d, o)
    known()
    token(5, x_down)
    em[c, own] = sm[c]
    en[c, 1] = sn[c]

    heard(5)
    token(6, y_up)
    token(8, y_down)
    heard(6)
    token(7, y_up)
    cs[24] = zero8
    tb[16] = jnp.zeros((cols, 128), F32)
    for s in range(2):
        vs[s, 24] = jnp.zeros((2 * cols, 256), BF16)
        em[s, 24] = zero8
        en[s, 3] = zero8

    def source(v, first, none):
        return jnp.where(v >= 0, jnp.clip(v - first, 0, none - 1), none)

    def forward(q, part):
        rows = pl.ds(part * 8, 8)
        return remote(ev.at[q, rows], rv.at[q, rows], f_send.at[q, part], f_recv.at[q, part], d, o)

    def forward_coords(q, core):
        land = cs.at[pl.ds(16 * q + 4 * core, 4)]
        return remote(land, land, g_send.at[q], g_recv.at[q], d, o)

    def pass_on():
        for q, leaf, _, there in sides:

            @pl.when(there)
            def _(q=q, leaf=leaf):
                for part in range(2):
                    columns_to(q, leaf, part).wait_recv()
                    forward(q, part).start()
                coords_to(q, leaf).wait_recv()
                forward_coords(q, c).start()

    def take_points():
        for q, _, _, there in sides:

            @pl.when(there)
            def _(q=q):
                for l in range(leaves):
                    vs[c, 16 * q + l] = stacked(ev[q, :, l * 256 : (l + 1) * 256])

        remote(vals, rv.at[2], f_send.at[2, 0], f_recv.at[2, 0], d, o).wait_recv()
        for l in range(leaves):
            vs[o, leaves + l] = stacked(rv[2, :, l * 256 : (l + 1) * 256])
        for q, _, _, there in sides:

            @pl.when(there)
            def _(q=q):
                forward_coords(q, o).wait_recv()
                forward(q, 0).wait_recv()
                forward(q, 1).wait_recv()
                for l in range(leaves):
                    vs[o, 16 * q + l] = stacked(rv[q, :, l * 256 : (l + 1) * 256])

    first = jnp.full((cols, 128), c, jnp.int32) == 0
    wide = jnp.full((cols, 256), c, jnp.int32) == 0

    def result(t):
        return remote(ns.at[t], nr.at[t], r_send.at[t], r_recv.at[t], d, o)

    def near(t, carry):
        l = c * 4 + t
        points = cs[leaves + l].T
        for k in range(3):
            bx[k, 0:128, :] = jnp.broadcast_to(points[:, k : k + 1], (128, 128))
            bx[k, 128:256, :] = jnp.broadcast_to(points[:, 3 + k : 4 + k], (128, 128))
        total = None
        for j in range(8):
            i = source(near_ref[l, j], (d - 1) * leaves, 24)
            rows = cs[i]
            his, los = [], []
            for h in range(2):
                r2 = None
                for k in range(3):
                    e = bx[k] - rows[3 * h + k : 3 * h + k + 1, :]
                    r2 = e * e if r2 is None else r2 + e * e
                hi, lo = split(lax.rsqrt(r2 + SOFTENING))
                his.append(hi)
                los.append(lo)
            v0, v1 = vs[0, i], vs[1, i]
            v2 = jnp.concatenate([v0[:cols], v1[:cols], v0[cols:], v1[cols:]], 0)
            term = dot3(v2, jnp.concatenate(his, 1), jnp.concatenate(los, 1), NT)
            total = term if total is None else total + term
        total = total * (1.0 / 16.0)
        a, b = total[:cols], total[cols:]
        nk[t] = jnp.where(wide, a, b)
        ns[t] = jnp.where(wide, b, a)
        result(t).start()
        return carry

    for copy in get_lists:
        copy.wait()
    pass_on()
    total = contrib
    for k in range(1, 8):
        remote(sc, zb.at[k], z_send.at[k], z_recv.at[k], d, o).wait_recv()
    for k in range(1, 8):
        total = total + zb[k]
    st[...] = total
    heard(8, 7)
    far_first = sorted(range(1, 16), key=lambda k: -(min(k // 4, 4 - k // 4) + min(k % 4, 4 - k % 4)))
    for k in far_first:
        send(st, tb.at[g], t_send.at[k], t_recv.at[k], chip(x + k // 4, y + k % 4, z), c)
    tb[g] = total

    def paired(load, i, j):
        rows = []
        for s in range(2):
            a, b = load(s, i), load(s, j)
            rows += [jnp.where(low, a, pltpu.roll(b, 64, 1)), jnp.where(low, pltpu.roll(a, 64, 1), b)]
        return jnp.concatenate(rows, 0)

    def coupled(load, index, blocks):
        slots = blocks.shape[0]
        picked = jnp.concatenate([paired(load, index(j), index(j + 1)) for j in range(0, slots, 2)], 1)
        return dot3(stacked(picked), *split(blocks.reshape(slots * 64, 128)), NN)

    for q, _, _, there in sides:

        @pl.when(there)
        def _(q=q):
            for h in range(2):
                land = pl.ds(16 * q, leaves)
                remote(sm.at[h], em.at[h, land], m_send.at[0, h], m_recv.at[2 * q, h], d, o).wait_recv()
                remote(sn.at[h], en.at[h, 2 * q], n_send.at[0, h], n_recv.at[2 * q, h], d, o).wait_recv()

    remote(sm.at[o], em.at[o, own], m_send.at[2, o], m_recv.at[1, o], d, o).wait_recv()
    remote(sn.at[o], en.at[o, 1], n_send.at[2, o], n_recv.at[1, o], d, o).wait_recv()
    for copy in (get_lcp, get_ncp):
        copy.wait()

    def keep(i, both):
        a, b = both[:cols], both[cols:]
        ox[i] = jnp.where(first, a, b)
        sx[i] = jnp.where(first, b, a)

    for l in range(leaves):
        keep(l, coupled(lambda s, i: em[s, i], lambda j: source(leaf_ref[l, j], (d - 1) * leaves, 24), lcp[l]))
    keep(leaves, coupled(lambda s, i: en[s, i], lambda j: source(node_ref[0, j], d - 1, 3), ncp[0]))
    send(sx, rx, x_send.at[0], x_recv.at[0], d, o)
    remote(tcp.at[o], tcp.at[o], x_send.at[1], x_recv.at[1], d, o).wait_recv()
    for j in range(4):
        for h in range(2):
            rows = pl.ds(j * 128 + h * 64, 64)
            tth[rows], ttl[rows] = split(tcp[h, j])

    take_points()
    lax.fori_loop(0, 4, near, 0)

    remote(sx, rx, x_send.at[0], x_recv.at[0], d, o).wait_recv()
    for k in range(1, 16):
        remote(st, tb.at[g], t_send.at[k], t_recv.at[k], d, o).wait_recv()
    picked = jnp.concatenate([tb[source(top_ref[j, g], 0, 16)] for j in range(4)], 1)
    top_local = dot3(stacked(picked), tth[...], ttl[...], NN)
    node_local = ox[leaves] + rx[leaves] + dot3(stacked(top_local), nth[...], ntl[...], NT)
    node2 = stacked(node_local)
    for l in range(leaves):
        leaf_local = ox[l] + rx[l] + dot3(node2, lth[l], ltl[l], NT)
        far = dot3(stacked(leaf_local), bh[l], bl[l], NT)
        out[:, l * 256 : (l + 1) * 256] = far
    for t in range(4):
        result(t).wait_recv()
    for l in range(leaves):
        t, span = l % 4, slice(l * 256, (l + 1) * 256)
        close = jnp.where(wide, nk[t], nr[t]) if l < 4 else jnp.where(wide, nr[t], nk[t])
        out[:, span] = out[:, span] + close
    for copy in sends:
        copy.wait_send()
    for q, leaf, there, _ in sides:

        @pl.when(there)
        def _(q=q, leaf=leaf):
            points = [coords_to(q, leaf), columns_to(q, leaf, 0), columns_to(q, leaf, 1)]
            for copy in (*points, *moments_to(q, leaf)):
                copy.wait_send()

    for q, _, _, there in sides:

        @pl.when(there)
        def _(q=q):
            forward(q, 0).wait_send()
            forward(q, 1).wait_send()
            forward_coords(q, c).wait_send()

    for t in range(4):
        result(t).wait_send()


def body(
    coords, values, leaf_basis, leaf_transfer, node_transfer, leaf_coupling, node_coupling, top_coupling,
    near_list, leaf_list, node_list, top_list,
):
    cols = values.shape[0]
    any_ref = pl.BlockSpec(memory_space=pl.ANY)
    vmem = pl.BlockSpec(memory_space=pltpu.VMEM)
    dma = pltpu.SemaphoreType.DMA
    return pl.pallas_call(
        kernel,
        out_shape=pltpu.VMEM(values.shape, F32),
        in_specs=[any_ref] * 12,
        out_specs=vmem,
        scratch_shapes=[
            pltpu.SMEM((8, 8), jnp.int32),
            pltpu.SMEM((8, 8), jnp.int32),
            pltpu.SMEM((1, 2), jnp.int32),
            pltpu.SMEM((4, 16), jnp.int32),
            pltpu.VMEM((3, 2048), F32),
            pltpu.VMEM((cols, 2048), F32),
            pltpu.VMEM((2, cols, 2048), F32),
            pltpu.VMEM((25, 8, 128), F32),
            pltpu.VMEM((3, cols, 2048), F32),
            pltpu.VMEM((2, 25, 2 * cols, 256), BF16),
            pltpu.VMEM((4, cols, 256), F32),
            pltpu.VMEM((4, cols, 256), F32),
            pltpu.VMEM((4, cols, 256), F32),
            pltpu.VMEM((3, 256, 128), F32),
            pltpu.VMEM((2, 25, 8, 128), F32),
            pltpu.VMEM((2, 4, 8, 128), F32),
            pltpu.VMEM((8, cols, 128), F32),
            pltpu.VMEM((17, cols, 128), F32),
            pltpu.VMEM((2, 8, 8, 128), F32),
            pltpu.VMEM((2, 8, 128), F32),
            pltpu.VMEM((cols, 128), F32),
            pltpu.VMEM((cols, 128), F32),
            pltpu.VMEM((8, 256, 128), F32),
            pltpu.VMEM((8, 128, 128), F32),
            pltpu.VMEM((1, 128, 128), F32),
            pltpu.VMEM((8, 8, 64, 128), F32),
            pltpu.VMEM((1, 2, 64, 128), F32),
            pltpu.VMEM((2, 4, 64, 128), F32),
            pltpu.VMEM((8, 256, 128), BF16),
            pltpu.VMEM((8, 256, 128), BF16),
            pltpu.VMEM((8, 128, 128), BF16),
            pltpu.VMEM((8, 128, 128), BF16),
            pltpu.VMEM((128, 128), BF16),
            pltpu.VMEM((128, 128), BF16),
            pltpu.VMEM((512, 128), BF16),
            pltpu.VMEM((512, 128), BF16),
            pltpu.VMEM((9, cols, 128), F32),
            pltpu.VMEM((9, cols, 128), F32),
            pltpu.VMEM((9, cols, 128), F32),
            dma((13,)),
            dma((2, 2)), dma((2, 2)), dma((2,)), dma((2,)),
            dma((3, 2)), dma((3, 2)), dma((3, 2)), dma((3, 2)),
            dma((8,)), dma((8,)), dma((16,)), dma((16,)),
            dma((2,)), dma((2,)), dma((3, 2)), dma((3, 2)), dma((2,)), dma((2,)), dma((4,)), dma((4,)), pltpu.SemaphoreType.REGULAR((9,)), pltpu.SemaphoreType.REGULAR((4,)),
        ],
        compiler_params=pltpu.CompilerParams(collective_id=0, has_side_effects=True),
    )(
        near_list, leaf_list, node_list, top_list.T, coords, values,
        leaf_basis, leaf_transfer, node_transfer, leaf_coupling, node_coupling, top_coupling,
    )


def solution(mesh):
    in_specs = (
        P(None, "leaf"),
        P("col", "leaf"),
        P("leaf", None, None),
        P("leaf", None, None),
        P("leaf", None, None),
        P("leaf", None, "col", None),
        P("leaf", None, "col", None),
        P(None, None, "col", None),
        P("leaf", None),
        P("leaf", None),
        P("leaf", None),
        P(),
    )
    return jax.shard_map(body, mesh=mesh, in_specs=in_specs, out_specs=P("col", "leaf"), check_vma=False)
```
